256 devices in a mesh: env: 4 (over x_lo, core), tm: 64 (over x_hi, z, y).
Axes of the slice: x: 4 (x_hi: 2, x_lo: 2; x = x_hi * 2 + x_lo), y: 4, z: 8, core: 2. Of those that a mesh axis runs over, the one named last changes fastest.
Arguments:
- hidden: bfloat16 [4, 64, 256, 1024], P('env', 'tm'), may hold values from -6 to 6
- done_step: int32 [4, 64], P('env', 'tm'), may hold values from 0 to 255
- alive: int32 [4, 64, 256], P('env', None, 'tm'), may hold values 0 or 1
- targets: float32 [4, 64, 256], P('env', None, 'tm'), may hold values from -6 to 6
- gain_t: float32 [1024], replicated, may hold values from 0.25 to 1.75
- w_qkv_t: bfloat16 [1024, 3072], replicated, may hold values from -5 to 5
- w_out_t: bfloat16 [1024, 1024], replicated, may hold values from -0.1875 to 0.1875
- gain_a: float32 [1024], replicated, may hold values from 0.25 to 1.75
- w_qkv_a: bfloat16 [1024, 3072], P('tm'), may hold values from -5 to 5
- w_out_a: bfloat16 [1024, 1024], P('tm'), may hold values from -0.1875 to 0.1875
- w_value: float32 [1024], replicated, may hold values from -0.1875 to 0.1875
Outputs:
- values: float32 [4, 64, 256], P('env', None, 'tm')
- input_grad: bfloat16 [4, 64, 256, 1024], P('env', 'tm')
- qkv_grad: float32 [1024, 3072], P('tm')
- out_grad: float32 [1024, 1024], P('tm')
The draws below stay inside these ranges and needn't reach their ends.
Inputs may be any that keep to these rules, and one draw needn't show every extreme that they name: `done_step`: the last step of an agent's first episode in the window; later steps form a new episode.
All inputs are finite; a program needn't handle non-finite values. No bound on the sum of `alive` on one device may be relied on, other than what follows from the above.
Results may differ from the reference program's by a relative error of at most 0.02.
Values may be sent and summed in bfloat16 or wider, within the bound.
A program may use at most 128 MiB of HBM per device.

```python
import math
import jax
import jax.numpy as jnp
from jax import lax

D = 1024
HEADS = 8
STEPS = 256
AGENTS = 64
ENVS = 4


def projection_draw(key):
    base = jax.random.normal(key, (D, 3 * D), jnp.float32) / math.sqrt(D)
    return jnp.clip(base, -5.0, 5.0)


def draw_w_qkv_t(key, part):
    return projection_draw(jax.random.fold_in(key, 11)).astype(jnp.bfloat16)


def draw_w_qkv_a(key, part):
    return projection_draw(jax.random.fold_in(key, 23)).astype(jnp.bfloat16)


def set_ends(result, stream_key, smallest, largest):
    spot = [jax.random.randint(jax.random.fold_in(stream_key, axis), (), 0, length) for axis, length in enumerate(result.shape)]
    main_axis = result.shape.index(max(result.shape))
    neighbour = spot[:main_axis] + [(spot[main_axis] + 1) % result.shape[main_axis]] + spot[main_axis + 1:]
    return result.at[tuple(spot)].set(smallest).at[tuple(neighbour)].set(largest)


def block_scale(own_key, shape, shards, low, high):
    factor_of, own = 1.0, jax.random.fold_in(own_key, 6)
    for axis_at, parts in shards:
        heights = jnp.exp(jax.random.uniform(jax.random.fold_in(own, axis_at), (parts,), jnp.float32, low / len(shards), high / len(shards)))
        factor_of = factor_of * jnp.repeat(heights, shape[axis_at] // parts).reshape([-1 if axis == axis_at else 1 for axis in range(len(shape))])
    return factor_of


def normal_values(stream_key, shape, spread, most, shards=(), held_as=jnp.bfloat16):
    drawn = spread * jax.random.normal(stream_key, shape, jnp.float32)
    if shards:
        drawn = drawn * block_scale(stream_key, shape, shards, -0.22, 0.18)
    return jnp.clip(drawn, -most, most).astype(held_as)


def setup_inputs(seed: int = 0) -> dict:
    splits = jax.random.split(jax.random.key(seed), 12)
    hidden = normal_values(splits[0], (ENVS, AGENTS, STEPS, D), 1.0, 6.0, ((0, 4), (1, 64)))
    done_step = set_ends(jax.random.randint(splits[1], (ENVS, AGENTS), 0, STEPS), jax.random.fold_in(splits[1], 1), 0, STEPS - 1).astype(jnp.int32)
    alive = set_ends((jax.random.randint(splits[2], (ENVS, AGENTS, STEPS), 0, 4) < 3).astype(jnp.int32), jax.random.fold_in(splits[2], 1), 0, 1)
    targets = normal_values(splits[3], (ENVS, AGENTS, STEPS), 1.0, 6.0, ((0, 4), (2, 64)), jnp.float32)
    gain_t = jnp.clip(1.0 + 0.15 * jax.random.normal(splits[4], (D,), jnp.float32), 0.25, 1.75)
    w_qkv_t = draw_w_qkv_t(jax.random.fold_in(splits[11], 71), 0)
    w_out_t = normal_values(splits[6], (D, D), D ** -0.5, 0.1875)
    gain_a = jnp.clip(1.0 + 0.15 * jax.random.normal(splits[7], (D,), jnp.float32), 0.25, 1.75)
    w_qkv_a = draw_w_qkv_a(jax.random.fold_in(splits[11], 71), 0)
    w_out_a = normal_values(splits[9], (D, D), D ** -0.5, 0.1875, ((0, 64),))
    w_value = normal_values(splits[10], (D,), D ** -0.5, 0.1875, (), jnp.float32)
    return {"hidden": hidden, "done_step": done_step, "alive": alive, "targets": targets, "gain_t": gain_t, "w_qkv_t": w_qkv_t, "w_out_t": w_out_t, "gain_a": gain_a, "w_qkv_a": w_qkv_a, "w_out_a": w_out_a, "w_value": w_value}


def norm_scale(rows, gain):
    return rows * lax.rsqrt(lax.optimization_barrier(jnp.mean(rows * rows, axis=-1, keepdims=True)) + 1e-06) * gain

def attend(qkv, allowed, head_count, layout):
    width = qkv.shape[-1] // 3
    size = width // head_count
    shape = qkv.shape[:-1] + (head_count, size)
    queries = qkv[..., :width].reshape(shape).astype(jnp.float32)
    key_rows = qkv[..., width:2 * width].reshape(shape).astype(jnp.float32)
    value_rows = qkv[..., 2 * width:].reshape(shape).astype(jnp.float32)
    if layout == 'temporal':
        score_form = 'bqhe,bkhe->bhqk'
        mix_form = 'bhqk,bkhe->bqhe'
    else:
        score_form = 'qbhe,kbhe->bhqk'
        mix_form = 'bhqk,kbhe->qbhe'
    scores = jnp.einsum(score_form, queries, key_rows) / math.sqrt(size)
    scores = jnp.where(allowed[:, None], scores, -1e+30)
    row_max = lax.optimization_barrier(jnp.max(scores, axis=-1, keepdims=True))
    weights = jnp.exp(scores - row_max)
    probs = (weights / lax.optimization_barrier(jnp.sum(weights, axis=-1, keepdims=True))).astype(jnp.bfloat16)
    mixed = jnp.einsum(mix_form, probs.astype(jnp.float32), value_rows)
    return mixed.reshape(qkv.shape[:-1] + (width,))

def temporal_block(rows, done, gain, w_qkv, w_out, head_count):
    batch, length, width = rows.shape
    rows_f = rows.astype(jnp.float32)
    normed = norm_scale(rows_f, gain).astype(jnp.bfloat16)
    qkv = jnp.dot(normed.reshape(-1, width), w_qkv, preferred_element_type=jnp.float32)
    qkv = qkv.astype(jnp.bfloat16).reshape(batch, length, 3 * width)
    positions = jnp.arange(length, dtype=jnp.int32)
    later = positions[None, :] > done[:, None]
    causal = positions[:, None] >= positions[None, :]
    allowed = causal[None] & (later[:, :, None] == later[:, None, :])
    mixed = attend(qkv, allowed, head_count, 'temporal').astype(jnp.bfloat16)
    added = jnp.dot(mixed.reshape(-1, width), w_out, preferred_element_type=jnp.float32)
    return (rows_f + added.reshape(batch, length, width)).astype(jnp.bfloat16)

def left_product(left, right):
    return lax.dot_general(left, right, (((0,), (0,)), ((), ())), preferred_element_type=jnp.float32)

def agent_step(lifted, alive_rows, target_rows, gain, w_qkv, w_out, w_value, head_count):
    agent_count, step_count, width = lifted.shape
    lifted_f = lifted.astype(jnp.float32)
    normed_f, norm_pull = jax.vjp(lambda rows: norm_scale(rows, gain), lifted_f)
    normed = normed_f.astype(jnp.bfloat16).reshape(-1, width)
    qkv = jnp.dot(normed, w_qkv, preferred_element_type=jnp.float32)
    qkv = qkv.astype(jnp.bfloat16).reshape(agent_count, step_count, 3 * width)
    living = alive_rows.T == 1
    allowed = living[:, None, :] | jnp.eye(agent_count, dtype=bool)[None]
    mixed_f, attend_pull = jax.vjp(lambda block: attend(block, allowed, head_count, 'agents'), qkv)
    mixed = mixed_f.astype(jnp.bfloat16).reshape(-1, width)
    added = jnp.dot(mixed, w_out, preferred_element_type=jnp.float32)
    top_rows = lifted_f + added.reshape(agent_count, step_count, width)
    predicted = lax.optimization_barrier(jnp.sum(top_rows * w_value, axis=-1))
    residual_err = 32.0 * alive_rows.astype(jnp.float32) * (predicted - target_rows)
    grad_top = residual_err[..., None] * w_value
    grad_rows = grad_top.astype(jnp.bfloat16).reshape(-1, width)
    grad_mixed = jnp.dot(grad_rows, w_out.T, preferred_element_type=jnp.float32)
    grad_qkv = attend_pull(grad_mixed.reshape(agent_count, step_count, width))[0]
    grad_qkv = grad_qkv.reshape(-1, 3 * width)
    grad_normed = jnp.dot(grad_qkv, w_qkv.T, preferred_element_type=jnp.float32)
    grad_lifted = grad_top + norm_pull(grad_normed.reshape(agent_count, step_count, width))[0]
    return (predicted, grad_lifted.astype(jnp.bfloat16), normed, grad_qkv, mixed, grad_rows)

def reference(hidden, done_step, alive, targets, gain_t, w_qkv_t, w_out_t, gain_a, w_qkv_a, w_out_a, w_value):
    predicted_all = []
    input_all = []
    qkv_total = jnp.zeros((D, 3 * D), jnp.float32)
    out_total = jnp.zeros((D, D), jnp.float32)
    for env_index in range(ENVS):
        done_rows = done_step[env_index]
        first, pull = jax.vjp(lambda rows: temporal_block(rows, done_rows, gain_t, w_qkv_t, w_out_t, HEADS), hidden[env_index])
        lifted = jnp.swapaxes(first, 0, 1)
        lifted = jnp.swapaxes(lifted, 0, 1)
        predicted, grad_lifted, normed, grad_qkv, mixed, grad_rows = agent_step(lifted, alive[env_index], targets[env_index], gain_a, w_qkv_a, w_out_a, w_value, HEADS)
        qkv_total = qkv_total + left_product(normed, grad_qkv)
        out_total = out_total + left_product(mixed, grad_rows)
        input_all.append(pull(grad_lifted)[0])
        predicted_all.append(predicted)
    return (jnp.stack(predicted_all), jnp.stack(input_all), qkv_total, out_total)
```

```python
import math

import jax
import jax.numpy as jnp
from jax import lax
from jax.sharding import PartitionSpec as P

HEADS = 8
HI = lax.Precision.HIGHEST


def norm_scale(rows, gain):
    return rows * lax.rsqrt(jnp.mean(rows * rows, axis=-1, keepdims=True) + 1e-06) * gain


def attend(qkv, allowed, head_count):
    width = qkv.shape[-1] // 3
    size = width // head_count
    shape = qkv.shape[:-1] + (head_count, size)
    queries = qkv[..., :width].reshape(shape)
    key_rows = qkv[..., width : 2 * width].reshape(shape)
    value_rows = qkv[..., 2 * width :].reshape(shape)
    scores = jnp.einsum("qhe,khe->hqk", queries, key_rows, preferred_element_type=jnp.float32)
    scores = jnp.where(allowed[None], scores / math.sqrt(size), -1e30)
    row_max = jnp.max(scores, axis=-1, keepdims=True)
    weights = jnp.exp(scores - row_max)
    probs = (weights / jnp.sum(weights, axis=-1, keepdims=True)).astype(jnp.bfloat16)
    mixed = jnp.einsum("hqk,khe->qhe", probs, value_rows, preferred_element_type=jnp.float32)
    return mixed.reshape(qkv.shape[:-1] + (width,))


def temporal_block(rows, done, gain, w_qkv, w_out, head_count):
    length, width = rows.shape
    rows_f = rows.astype(jnp.float32)
    normed = norm_scale(rows_f, gain).astype(jnp.bfloat16)
    qkv = jnp.dot(normed, w_qkv, preferred_element_type=jnp.float32).astype(jnp.bfloat16)
    positions = jnp.arange(length, dtype=jnp.int32)
    later = positions > done
    allowed = (positions[:, None] >= positions[None, :]) & (later[:, None] == later[None, :])
    mixed = attend(qkv, allowed, head_count).astype(jnp.bfloat16)
    added = jnp.dot(mixed, w_out, preferred_element_type=jnp.float32)
    return (rows_f + added).astype(jnp.bfloat16)


def left_product(left, right):
    return lax.dot_general(
        left, right, (((0,), (0,)), ((), ())), preferred_element_type=jnp.float32
    )


def agent_step(lifted, alive_rows, target_rows, gain, w_qk, z, w_value, head_count):
    agent_count, step_count, width = lifted.shape
    size = width // head_count
    lifted_f = lifted.astype(jnp.float32)
    normed_f, norm_pull = jax.vjp(lambda rows: norm_scale(rows, gain), lifted_f)
    normed = normed_f.astype(jnp.bfloat16).reshape(-1, width)
    qk = jnp.dot(normed, w_qk, preferred_element_type=jnp.float32).astype(jnp.bfloat16)
    qk = qk.reshape(agent_count, step_count, 2, head_count, size)
    q, k = qk[:, :, 0], qk[:, :, 1]
    s = jnp.dot(normed.astype(jnp.float32), z, precision=HI)
    s = s.reshape(agent_count, step_count, head_count).transpose(1, 2, 0)
    living = alive_rows.T == 1
    allowed = living[:, None, :] | jnp.eye(agent_count, dtype=bool)[None]
    scores = jnp.einsum("qbhe,kbhe->bhqk", q, k, preferred_element_type=jnp.float32)
    scores = jnp.where(allowed[:, None], scores / math.sqrt(size), -1e30)
    weights = jnp.exp(scores - jnp.max(scores, axis=-1, keepdims=True))
    probs = weights / jnp.sum(weights, axis=-1, keepdims=True)
    pv = jnp.sum(probs * s[:, :, None, :], axis=-1)
    predicted = jnp.sum(lifted_f * w_value, axis=-1) + jnp.sum(pv, axis=1).T
    err = 32.0 * alive_rows.astype(jnp.float32) * (predicted - target_rows)
    weighted = probs * err.T[:, None, :, None]
    t = jnp.sum(weighted, axis=2)
    ds = weighted * (s[:, :, None, :] - pv[..., None]) * (1.0 / math.sqrt(size))
    ds = ds.astype(jnp.bfloat16)
    dq = jnp.einsum("bhqk,kbhe->qbhe", ds, k, preferred_element_type=jnp.float32)
    dk = jnp.einsum("bhqk,qbhe->kbhe", ds, q, preferred_element_type=jnp.float32)
    dqk = jnp.stack([dq, dk], axis=2).astype(jnp.bfloat16).reshape(-1, 2 * width)
    t = t.transpose(2, 0, 1).reshape(-1, head_count)
    grad_normed = jnp.dot(dqk, w_qk.T, preferred_element_type=jnp.float32)
    grad_normed = grad_normed + jnp.dot(t, z.T, precision=HI)
    grad_top = err[..., None] * w_value
    grad_lifted = grad_top + norm_pull(grad_normed.reshape(agent_count, step_count, width))[0]
    return (predicted, grad_lifted.astype(jnp.bfloat16), normed, dqk, t)


def per_device(
    hidden, done_step, alive, targets, gain_t, w_qkv_t, w_out_t, gain_a, w_qkv_a, w_out_a, w_value
):
    width = hidden.shape[-1]
    size = width // HEADS
    local_rows = hidden[0, 0]
    done = done_step[0, 0]
    v = lax.all_gather(
        jnp.sum(w_out_a.astype(jnp.float32) * w_value, axis=1), "tm", axis=0, tiled=True
    )
    w_v = w_qkv_a[:, 2 * width :].astype(jnp.float32)
    z = jnp.sum((w_v * v).reshape(-1, HEADS, size), axis=-1)
    z = lax.all_gather(z, "tm", axis=0, tiled=True)
    w_qk = lax.all_gather(w_qkv_a[:, : 2 * width], "tm", axis=0, tiled=True)
    first, pull = jax.vjp(
        lambda rows: temporal_block(rows, done, gain_t, w_qkv_t, w_out_t, HEADS), local_rows
    )
    lifted = lax.all_to_all(first[None], "tm", split_axis=1, concat_axis=0, tiled=True)
    predicted, grad_lifted, normed, dqk, t = agent_step(
        lifted, alive[0], targets[0], gain_a, w_qk, z, w_value, HEADS
    )
    returned = lax.all_to_all(grad_lifted, "tm", split_axis=0, concat_axis=1, tiled=True)
    terms = left_product(normed, dqk).astype(jnp.bfloat16)
    u_terms = lax.dot_general(
        normed.astype(jnp.float32), t, (((0,), (0,)), ((), ())), precision=HI
    )
    summed = lax.psum_scatter(terms, "tm", scatter_dimension=0, tiled=True)
    qk_grad = lax.psum(summed, "env").astype(jnp.float32)
    u_mine = lax.psum(u_terms, ("env", "tm"))
    u_mine = lax.dynamic_slice_in_dim(
        u_mine, lax.axis_index("tm") * w_v.shape[0], w_v.shape[0], 0
    )
    u_wide = jnp.repeat(u_mine, size, axis=1)
    v_grad = u_wide * v
    mixed_err = lax.psum(jnp.sum(u_wide * w_v, axis=0), "tm")
    mixed_err = lax.dynamic_slice_in_dim(
        mixed_err, lax.axis_index("tm") * w_out_a.shape[0], w_out_a.shape[0], 0
    )
    out_grad = mixed_err[:, None] * w_value
    qkv_grad = jnp.concatenate([qk_grad, v_grad], axis=1)
    input_grad = pull(returned[0])[0]
    return (predicted[None], input_grad[None, None], qkv_grad, out_grad)


def solution(mesh):
    in_specs = (
        P("env", "tm", None, None),
        P("env", "tm"),
        P("env", None, "tm"),
        P("env", None, "tm"),
        P(),
        P(),
        P(),
        P(),
        P("tm", None),
        P("tm", None),
        P(),
    )
    out_specs = (P("env", None, "tm"), P("env", "tm", None, None), P("tm", None), P("tm", None))
    return jax.shard_map(
        per_device, mesh=mesh, in_specs=in_specs, out_specs=out_specs, check_vma=False
    )
```

```python
import math

import jax
import jax.numpy as jnp
from jax import lax
from jax.experimental import pallas as pl
from jax.experimental.pallas import tpu as pltpu
from jax.sharding import PartitionSpec as P

F32, BF16 = jnp.float32, jnp.bfloat16
HEADS, D, STEPS, AGENTS = 8, 1024, 256, 64
HD = D // HEADS
SCALE = 1.0 / math.sqrt(HD)
CUT = 512
WIDE = D + 128
NEG = -1e30


def dot(a, b, ca, cb):
    return lax.dot_general(a, b, (((ca,), (cb,)), ((), ())), preferred_element_type=F32)


def nn(a, b):
    return dot(a, b, 1, 0)


def nt(a, b):
    return dot(a, b, 1, 1)


def tn(a, b):
    return dot(a, b, 0, 0)


def iota(shape, axis):
    return lax.broadcasted_iota(jnp.int32, shape, axis)


def split(x):
    high = x.astype(BF16)
    return high, (x - high.astype(F32)).astype(BF16)


def pick(condition):
    return jnp.where(condition, 1.0, 0.0).astype(BF16)


def step_to_block(flip):
    i, c = iota((256, 256), 1 if flip else 0), iota((256, 256), 0 if flip else 1)
    return pick(((i // 4) % 4 == c // 64) & (c % 64 == (i // 16) * 4 + i % 4))


def block_to_agent(flip):
    i, c = iota((256, 256), 1 if flip else 0), iota((256, 256), 0 if flip else 1)
    return pick((i % 16 == c // 16) & (i // 16 == c % 16))


def kernel(
    hidden_h, done_v, rows_v, gain_t_v, wqkv_h, wout_h, gain_a_v, wqkva_v, wouta_v, wval_v,
    values_o, igrad_o, qkvg_o, outg_o,
    hid, wqkv, wout, norm_t, qkv, prob_t, mixed, stage1, a1, r1, xr,
    w2, vb, zb, ub, z128, na, nat, qk, prob_a, dqk, trow, gnorm, stage2, a2, r2, gh,
    tb, rx, cws, cwr, ccs, ccr, sa, ya, yb, sb, zbuf, fx, xbuf, fin, lbuf, cbuf, urow,
    lsem, gs, gr, as1, ar1, as2, ar2, vs, vr, zs, zr, us, ur, rs, rr, own_sem,
):
    me, env = lax.axis_index("tm"), lax.axis_index("env")
    core = env % 2
    xh, z, y = me // 32, (me // 4) % 8, me % 4
    core_id = {"env": env + 1 - 2 * core}
    lo_id = {"env": (env + 2) % 4}

    def tm_at(xh_, z_, y_):
        return {"tm": xh_ * 32 + z_ * 4 + y_}

    x_id = tm_at(1 - xh, z, y)

    def send(src, dst, sems, k, where):
        copy = pltpu.make_async_remote_copy(
            src_ref=src, dst_ref=dst, send_sem=sems[0].at[k], recv_sem=sems[1].at[k],
            device_id=where, device_id_type=pl.DeviceIdType.MESH,
        )
        copy.start()
        return copy

    def spread(body):
        def step(i, carry):
            body(lax.rem(me + i, 64))
            return carry
        lax.fori_loop(1, 64, step, 0)

    loads = [pltpu.make_async_copy(hidden_h, hid, lsem.at[0])]
    for j in range(6):
        at = (slice(None), slice(512 * j, 512 * j + 512))
        loads.append(pltpu.make_async_copy(wqkv_h.at[at], wqkv.at[at], lsem.at[1 + j]))
    loads.append(pltpu.make_async_copy(wout_h, wout, lsem.at[7]))
    for load in loads:
        load.start()

    barrier = pltpu.get_barrier_semaphore()

    def greet(peer):
        pl.semaphore_signal(
            barrier, inc=1, device_id={"tm": peer}, device_id_type=pl.DeviceIdType.MESH
        )

    spread(greet)
    for i in (1, 2, 3):
        pl.semaphore_signal(
            barrier, inc=1, device_id={"env": (env + i) % 4}, device_id_type=pl.DeviceIdType.MESH
        )

    w_value = wval_v[...]
    lane_off = (me % 8) * 16
    spot = iota((16, 128), 1) == iota((16, 128), 0) + lane_off

    def to_lanes(column):
        return jnp.sum(jnp.where(spot, column, 0.0), axis=0, keepdims=True)

    own_rows = pl.ds(pl.multiple_of(y * 16, 16), 16)
    mine = wqkva_v[:, :D]
    other = wqkva_v[:, D : 2 * D]
    w2[core, xh, z, own_rows, :] = jnp.where(core == 0, mine, other)
    v_part = jnp.sum(wouta_v[...].astype(F32) * w_value, axis=1, keepdims=True)
    vb[me] = to_lanes(v_part)

    pl.semaphore_wait(barrier, 66)

    G, V, Z, U, R = (gs, gr), (vs, vr), (zs, zr), (us, ur), (rs, rr)
    a_cols, b_cols = pl.ds(0, 512), pl.ds(512, 512)

    def put_v(peer):
        send(vb.at[me], vb.at[me], V, 0, {"tm": peer})

    def put_z(peer):
        send(zb.at[me], zb.at[me], Z, 0, {"tm": peer})

    def put_u(peer):
        row = peer // 8
        send(urow.at[row], ub.at[me], U, 0, {"tm": peer})

    def all_of(ref, sems, n):
        return pltpu.make_async_remote_copy(
            src_ref=ref.at[pl.ds(0, n)], dst_ref=ref.at[pl.ds(0, n)], send_sem=sems[0].at[0],
            recv_sem=sems[1].at[0], device_id=x_id, device_id_type=pl.DeviceIdType.MESH,
        )

    def piece(xs, zs_, rows, cols):
        return w2.at[core, xs, zs_, rows, cols]

    whole = pl.ds(0, 64)
    both = pl.ds(0, 2)
    every = pl.ds(0, 8)
    live = {}

    def relay(name, k, ref, where):
        live[name] = send(ref, ref, G, k, where)

    def g_x():
        relay("x", 0, piece(xh, z, own_rows, pl.ds(0, D)), x_id)

    def g_yz():
        live["x"].wait()
        for i in (1, 2, 3):
            relay(("ya", i), i, piece(both, z, own_rows, a_cols), tm_at(xh, z, (y + i) % 4))
        for i in range(1, 8):
            relay(("zb", i), 3 + i, piece(both, z, own_rows, b_cols), tm_at(xh, (z + i) % 8, y))

    def ring(k):
        if k <= 4:
            at = (z + 9 - k) % 8
            relay(("cw", k), 10 + k, piece(both, at, whole, a_cols), tm_at(xh, (z + 1) % 8, y))
        if k <= 3:
            at = (z + k - 1) % 8
            relay(("cc", k), 14 + k, piece(both, at, whole, a_cols), tm_at(xh, (z + 7) % 8, y))

    def to_core(k, ref):
        relay(("core", k), 21 + k, ref, core_id)

    def g_ring1():
        for i in (1, 2, 3):
            live[("ya", i)].wait()
        ring(1)
        to_core(0, piece(both, z, whole, a_cols))

    def g_b():
        for i in range(1, 8):
            live[("zb", i)].wait()
        for i in (1, 2, 3):
            relay(
                ("yb", i), 17 + i, piece(both, every, own_rows, b_cols), tm_at(xh, z, (y + i) % 4)
            )
        to_core(1, piece(both, every, own_rows, b_cols))

    def g_ring(k):
        live[("cw", k)].wait()
        if k <= 3:
            live[("cc", k)].wait()
        if k < 4:
            ring(k + 1)
        to_core(2 * k, piece(both, (z + 8 - k) % 8, whole, a_cols))
        if k <= 3:
            to_core(2 * k + 1, piece(both, (z + k) % 8, whole, a_cols))

    def g_b_end():
        for i in (1, 2, 3):
            live[("yb", i)].wait()
            rows = pl.ds(pl.multiple_of(((y + 4 - i) % 4) * 16, 16), 16)
            to_core(8 + i, piece(both, every, rows, b_cols))

    def v_ready():
        all_of(vb, V, 63).wait()

    def make_z():
        v_ready()
        v8 = jnp.sum(vb[...].reshape(8, 8, 128), axis=1)
        rows = []
        for h in range(HEADS):
            w_v = wqkva_v[:, 2 * D + h * HD : 2 * D + (h + 1) * HD].astype(F32)
            col = jnp.sum(w_v * v8[h : h + 1, :], axis=1, keepdims=True)
            rows.append(to_lanes(col))
        zb[me] = jnp.concatenate(rows, axis=0)
        spread(put_z)
        return v8

    g_x()
    spread(put_v)

    loads[0].wait()
    x = hid[...].astype(F32)
    inv_t = lax.rsqrt(jnp.mean(x * x, axis=1, keepdims=True) + 1e-6)
    norm_t[...] = (x * inv_t * gain_t_v[...]).astype(BF16)
    for j in range(6):
        loads[1 + j].wait()
        at = slice(512 * j, 512 * j + 512)
        qkv[:, at] = nn(norm_t[...], wqkv[:, at]).astype(BF16)
        if j == 0:
            g_yz()
        if j == 2:
            g_ring1()
        if j == 4:
            g_b()
    done = done_v[...]
    ri, ci = iota((STEPS, STEPS), 0), iota((STEPS, STEPS), 1)
    allowed_t = (ri >= ci) & ((ri > done) == (ci > done))
    v8 = None
    for h in range(HEADS):
        at = slice(h * HD, (h + 1) * HD)
        s = nt(qkv[:, at], qkv[:, D + h * HD : D + (h + 1) * HD]) * SCALE
        s = jnp.where(allowed_t, s, NEG)
        e = jnp.exp(s - jnp.max(s, axis=1, keepdims=True))
        p = (e / jnp.sum(e, axis=1, keepdims=True)).astype(BF16)
        prob_t[h] = p
        mixed[:, at] = nn(p, qkv[:, 2 * D + h * HD : 2 * D + (h + 1) * HD]).astype(BF16)
        if h == 1:
            v8 = make_z()
        if h == 2:
            g_ring(1)
        if h == 5:
            g_ring(2)
    loads[7].wait()
    turn = step_to_block(False)
    for q in range(4):
        at = slice(256 * q, 256 * q + 256)
        h1 = (hid[:, at].astype(F32) + nn(mixed[...], wout[:, at])).astype(BF16)
        for j in range(4):
            stage1[j, q * 64 : q * 64 + 64, :] = h1[j * 64 : j * 64 + 64, :]
    for j in range(4):
        a1[j * 256 : j * 256 + 256, :] = nn(turn, stage1[j]).astype(BF16)

    def block(peer):
        return pl.ds(pl.multiple_of(peer * 16, 16), 16)

    def put_1(peer):
        send(a1.at[block(peer)], r1.at[block(me)], (as1, ar1), 0, {"tm": peer})

    spread(put_1)
    r1[block(me), :] = a1[block(me), :]
    g_ring(3)
    g_ring(4)
    g_b_end()

    all_of(zb, Z, 63).wait()
    zt = jnp.concatenate(
        [jnp.sum(zb[8 * j : 8 * j + 8], axis=0) for j in range(8)], axis=1
    )
    z_hi, z_lo = split(zt)
    z128[...] = jnp.zeros((128, D), BF16)
    z128[0:16, :] = jnp.concatenate([z_hi, z_hi], axis=0)
    z128[16:32, :] = jnp.concatenate([z_lo, jnp.zeros_like(z_lo)], axis=0)

    def wait_all(src, dst, sems):
        pltpu.make_async_remote_copy(
            src_ref=src.at[pl.ds(0, 1008)], dst_ref=dst.at[pl.ds(0, 1008)], send_sem=sems[0].at[0],
            recv_sem=sems[1].at[0], device_id=x_id, device_id_type=pl.DeviceIdType.MESH,
        ).wait()

    wait_all(a1, r1, (as1, ar1))

    unturn = block_to_agent(False)
    for j in range(4):
        got = nn(unturn, r1[j * 256 : j * 256 + 256, :]).astype(BF16)
        for q in range(4):
            for s in range(4):
                i = (q * 4 + s) * 16
                xr[s * 64 + j * 16 : s * 64 + j * 16 + 16, q * 256 : q * 256 + 256] = got[
                    i : i + 16, :
                ]
    xa = xr[...].astype(F32)
    inv_a = lax.rsqrt(jnp.mean(xa * xa, axis=1, keepdims=True) + 1e-6)
    h1_value = jnp.sum(xa * w_value, axis=1, keepdims=True)
    normed = xa * inv_a * gain_a_v[...]
    na[...] = normed.astype(BF16)
    for j in range(4):
        nat[j * 256 : j * 256 + 256, :] = normed[:, j * 256 : j * 256 + 256].T.astype(BF16)
    for k in range(12):
        live[("core", k)].wait()
    for c in range(2):
        for i in range(2):
            w = w2[c, :, :, :, 512 * i : 512 * i + 512].reshape(D, 512)
            at = c * D + 512 * i
            qk[:, at : at + 512] = nn(na[...], w).astype(BF16)
    s_rows = nt(z128[0:32, :], na[...])
    s_rows = s_rows[0:8] + s_rows[16:24]
    diag = ri == ci
    alive_row, target_row = rows_v[0:1, :], rows_v[1:2, :]

    def to_column(row):
        return jnp.sum(jnp.where(diag, row, 0.0), axis=1, keepdims=True)

    alive_col, target_col = to_column(alive_row), to_column(target_row)
    half = iota((128, 128), 0), iota((128, 128), 1)
    same_step = (half[0] // 64) == (half[1] // 64)
    sums = []
    for p in range(2):
        rows = slice(128 * p, 128 * p + 128)
        seen = same_step & ((alive_row[:, rows] == 1.0) | (half[0] == half[1]))
        total = jnp.zeros((128, 1), F32)
        for h in range(HEADS):
            at = slice(h * HD, (h + 1) * HD)
            s = nt(qk[rows, at], qk[rows, D + h * HD : D + (h + 1) * HD]) * SCALE
            s = jnp.where(seen, s, NEG)
            e = jnp.exp(s - jnp.max(s, axis=1, keepdims=True))
            e = e / jnp.sum(e, axis=1, keepdims=True)
            prob_a[h, p] = e
            total = total + jnp.sum(e * s_rows[h : h + 1, rows], axis=1, keepdims=True)
        sums.append(total)
    predicted = h1_value + jnp.concatenate(sums, axis=0)
    err = 32.0 * alive_col * (predicted - target_col)
    values_o[...] = jnp.sum(jnp.where(diag, predicted, 0.0), axis=0, keepdims=True)
    for p in range(2):
        rows = slice(128 * p, 128 * p + 128)
        for h in range(HEADS):
            at, at_k = slice(h * HD, (h + 1) * HD), slice(D + h * HD, D + (h + 1) * HD)
            e = prob_a[h, p]
            s_row = s_rows[h : h + 1, rows]
            pv = jnp.sum(e * s_row, axis=1, keepdims=True)
            weighted = e * err[rows, :]
            trow[h : h + 1, rows] = jnp.sum(weighted, axis=0, keepdims=True)
            ds = weighted * (s_row - pv) * SCALE
            dqk[rows, at] = nn(ds.astype(BF16), qk[rows, at_k]).astype(BF16)
            dqk[rows, at_k] = nn(ds.T.astype(BF16), qk[rows, at]).astype(BF16)
    t_hi = trow[...].astype(BF16).astype(F32)
    t_lo = trow[...] - t_hi
    t_all = jnp.concatenate([t_hi, t_lo, t_hi, jnp.zeros((104, STEPS), F32)], axis=0)
    t_col = t_all.T.astype(BF16)
    for i in range(4):
        at = slice(256 * i, 256 * i + 256)
        part = nn(t_col, z128[:, at])
        for c in range(2):
            w = w2[c, i // 2, 4 * (i % 2) : 4 * (i % 2) + 4].reshape(256, D)
            part = part + nt(dqk[:, c * D : c * D + D], w)
        gnorm[:, at] = part * gain_a_v[:, at]
    gy = gnorm[...]
    xa = xr[...].astype(F32)
    pull = jnp.mean(xa * gy, axis=1, keepdims=True) * (inv_a * inv_a * inv_a)
    grad = (err * w_value + gy * inv_a - xa * pull).astype(BF16)
    turn = block_to_agent(True)
    for j in range(4):
        for q in range(4):
            for s in range(4):
                i = (q * 4 + s) * 16
                stage2[i : i + 16, j * 256 : j * 256 + 256] = grad[
                    s * 64 + j * 16 : s * 64 + j * 16 + 16, q * 256 : q * 256 + 256
                ]
    for j in range(4):
        a2[j * 256 : j * 256 + 256, :] = nn(turn, stage2[:, j * 256 : j * 256 + 256]).astype(BF16)

    def put_2(peer):
        send(a2.at[block(peer)], r2.at[block(me)], (as2, ar2), 0, {"tm": peer})

    spread(put_2)
    r2[block(me), :] = a2[block(me), :]

    u_term = nn(nat[...], t_col).astype(BF16).reshape(2, 8, 64, 128)
    for c in range(2):
        for i in range(2):
            at = slice(512 * i, 512 * i + 512)
            part = nn(nat[...], dqk[:, c * D + 512 * i : c * D + 512 * i + 512])
            tb[c, :, :, :, at] = part.astype(BF16).reshape(2, 8, 64, 512)
        tb[c, :, :, :, D:WIDE] = u_term
    to_other = send(tb.at[1 - core], rx, R, 0, core_id)

    wait_all(a2, r2, (as2, ar2))
    unturn = step_to_block(True)
    for j in range(4):
        got = nn(unturn, r2[j * 256 : j * 256 + 256, :]).astype(BF16)
        for q in range(4):
            gh[j * 64 : j * 64 + 64, q * 256 : q * 256 + 256] = got[q * 64 : q * 64 + 64, :]

    cut_a, cut_b = pl.ds(0, CUT), pl.ds(CUT, WIDE - CUT)

    def r_start():
        to_other.wait()
        for i in range(2):
            for j in range(8):
                rx[i, j] = rx[i, j] + tb[core, i, j]
        live["cw1"] = send(
            rx.at[both, (z + 4) % 8, whole, cut_a], cwr.at[0], R, 1, tm_at(xh, (z + 1) % 8, y)
        )
        live["cc1"] = send(
            rx.at[both, (z + 5) % 8, whole, cut_a], ccr.at[0], R, 5, tm_at(xh, (z + 7) % 8, y)
        )
        for i in (1, 2, 3):
            there = (y + i) % 4
            rows = pl.ds(pl.multiple_of(there * 16, 16), 16)
            live[("yb2", i)] = send(
                rx.at[both, every, rows, cut_b], yb.at[i - 1], R, 7 + i, tm_at(xh, z, there)
            )

    def r_ring(k):
        live[f"cw{k - 1}"].wait()
        cws[k - 2] = cwr[k - 2] + rx[:, (z + 5 - k) % 8, :, 0:CUT]
        live[f"cw{k}"] = send(cws.at[k - 2], cwr.at[k - 1], R, k, tm_at(xh, (z + 1) % 8, y))
        if k <= 3:
            live[f"cc{k - 1}"].wait()
            ccs[k - 2] = ccr[k - 2] + rx[:, (z + 4 + k) % 8, :, 0:CUT]
            live[f"cc{k}"] = send(ccs.at[k - 2], ccr.at[k - 1], R, 4 + k, tm_at(xh, (z + 7) % 8, y))

    def r_b():
        for i in (1, 2, 3):
            live[("yb2", i)].wait()
        for i in range(2):
            for j in range(8):
                total = rx[i, j, own_rows, CUT:WIDE].astype(F32)
                for k in range(3):
                    total = total + yb[k, i, j].astype(F32)
                sb[i, j] = total.astype(BF16)
        for i in range(1, 8):
            there = (z + i) % 8
            live[("zb2", i)] = send(
                sb.at[both, there], zbuf.at[i - 1], R, 10 + i, tm_at(xh, there, y)
            )

    def r_a_end():
        live["cw4"].wait()
        live["cc3"].wait()
        total = cwr[3].astype(F32) + ccr[2].astype(F32) + rx[:, z, :, 0:CUT].astype(F32)
        sa[...] = total.astype(BF16)
        for i in (1, 2, 3):
            there = (y + i) % 4
            rows = pl.ds(pl.multiple_of(there * 16, 16), 16)
            live[("ya2", i)] = send(
                sa.at[both, rows], ya.at[i - 1], R, 17 + i, tm_at(xh, z, there)
            )

    def r_x():
        for i in range(1, 8):
            live[("zb2", i)].wait()
        total = sb[:, z].astype(F32)
        for k in range(7):
            total = total + zbuf[k].astype(F32)
        fx[:, :, CUT:WIDE] = total
        for i in (1, 2, 3):
            live[("ya2", i)].wait()
        total = sa[:, own_rows, :].astype(F32)
        for k in range(3):
            total = total + ya[k].astype(F32)
        fx[:, :, 0:CUT] = total
        live["x2"] = send(fx.at[1 - xh], xbuf, R, 21, x_id)

    def r_lo():
        live["x2"].wait()
        fin[...] = fx[xh] + xbuf[...]
        live["lo"] = send(fin, lbuf, R, 22, lo_id)

    def r_core():
        live["lo"].wait()
        total = fin[...] + lbuf[...]
        cbuf[core] = total[:, 0:D]
        live["core2"] = send(cbuf.at[core], cbuf.at[core], R, 23, core_id)
        u = total[:, D : D + 8] + total[:, D + 8 : D + 16]
        wide = jnp.concatenate(
            [jnp.broadcast_to(u[:, h : h + 1], (16, HD)) for h in range(HEADS)], axis=1
        )
        v_wide = jnp.concatenate([v8[h : h + 1, :] for h in range(HEADS)], axis=1)
        qkvg_o[:, 2 * D : 3 * D] = wide * v_wide
        weighted = jnp.sum(wide * wqkva_v[:, 2 * D : 3 * D].astype(F32), axis=0, keepdims=True)
        for j in range(8):
            urow[j] = weighted[:, 128 * j : 128 * j + 128]
        ub[me] = urow[me // 8]
        spread(put_u)

    def r_end():
        live["core2"].wait()
        qkvg_o[:, 0:D] = cbuf[0]
        qkvg_o[:, D : 2 * D] = cbuf[1]
        all_of(ub, U, 63).wait()
        row = jnp.sum(ub[...].reshape(64, 128), axis=0, keepdims=True)
        column = jnp.sum(jnp.where(spot, row, 0.0), axis=1, keepdims=True)
        outg_o[...] = column * w_value

    r_start()
    after = {1: lambda: r_ring(2), 3: lambda: r_ring(3), 5: lambda: (r_ring(4), r_b()), 7: r_a_end}
    for h in range(HEADS):
        at = slice(h * HD, (h + 1) * HD)
        at_k, at_v = slice(D + h * HD, D + (h + 1) * HD), slice(2 * D + h * HD, 2 * D + (h + 1) * HD)
        gm = nt(gh[...], wout[at, :]).astype(BF16)
        p = prob_t[h]
        pf = p.astype(F32)
        dp = nt(gm, qkv[:, at_v])
        ds = (pf * (dp - jnp.sum(pf * dp, axis=1, keepdims=True)) * SCALE)
        q_h, k_h = qkv[:, at], qkv[:, at_k]
        qkv[:, at_v] = nn(pf.T.astype(BF16), gm).astype(BF16)
        qkv[:, at] = nn(ds.astype(BF16), k_h).astype(BF16)
        qkv[:, at_k] = nn(ds.T.astype(BF16), q_h).astype(BF16)
        if h in after:
            after[h]()
    after = {1: r_x, 2: r_lo, 3: r_core}
    for i in range(4):
        at = slice(256 * i, 256 * i + 256)
        gnorm[:, at] = nt(qkv[...], wqkv[at, :]) * gain_t_v[:, at]
        if i in after:
            after[i]()
    gy = gnorm[...]
    x = hid[...].astype(F32)
    inv_t = lax.rsqrt(jnp.mean(x * x, axis=1, keepdims=True) + 1e-6)
    pull = jnp.mean(x * gy, axis=1, keepdims=True) * (inv_t * inv_t * inv_t)
    igrad_o[...] = (gh[...].astype(F32) + gy * inv_t - x * pull).astype(BF16)
    r_end()


def per_device(
    hidden, done_step, alive, targets, gain_t, w_qkv_t, w_out_t, gain_a, w_qkv_a, w_out_a, w_value
):
    rows = jnp.stack([alive[0].astype(F32).T.reshape(-1), targets[0].T.reshape(-1)])
    vmem = pl.BlockSpec(memory_space=pltpu.VMEM)
    away = pl.BlockSpec(memory_space=pl.ANY)
    mem = pltpu.VMEM
    dma = pltpu.SemaphoreType.DMA
    scratch = [
        mem((STEPS, D), BF16), mem((D, 3 * D), BF16), mem((D, D), BF16), mem((STEPS, D), BF16),
        mem((STEPS, 3 * D), BF16), mem((HEADS, STEPS, STEPS), BF16), mem((STEPS, D), BF16),
        mem((4, 256, 256), BF16), mem((1024, 256), BF16), mem((1024, 256), BF16),
        mem((STEPS, D), BF16),
        mem((2, 2, 8, 64, D), BF16), mem((64, 1, 128), F32), mem((64, 8, 128), F32),
        mem((64, 1, 128), F32), mem((128, D), BF16), mem((STEPS, D), BF16), mem((D, STEPS), BF16),
        mem((STEPS, 2 * D), BF16), mem((HEADS, 2, 128, 128), F32), mem((STEPS, 2 * D), BF16),
        mem((HEADS, STEPS), F32), mem((STEPS, D), F32), mem((256, 1024), BF16),
        mem((1024, 256), BF16), mem((1024, 256), BF16), mem((STEPS, D), BF16),
        mem((2, 2, 8, 64, WIDE), BF16), mem((2, 8, 64, WIDE), BF16), mem((3, 2, 64, CUT), BF16),
        mem((4, 2, 64, CUT), BF16), mem((2, 2, 64, CUT), BF16), mem((3, 2, 64, CUT), BF16),
        mem((2, 64, CUT), BF16), mem((3, 2, 16, CUT), BF16), mem((3, 2, 8, 16, WIDE - CUT), BF16),
        mem((2, 8, 16, WIDE - CUT), BF16), mem((7, 2, 16, WIDE - CUT), BF16),
        mem((2, 16, WIDE), F32), mem((16, WIDE), F32), mem((16, WIDE), F32), mem((16, WIDE), F32),
        mem((2, 16, D), F32), mem((8, 1, 128), F32),
        dma((8,)), dma((33,)), dma((33,)), dma((1,)), dma((1,)), dma((1,)), dma((1,)), dma((1,)),
        dma((1,)), dma((1,)), dma((1,)), dma((1,)), dma((1,)), dma((24,)), dma((24,)), dma((1,)),
    ]
    values, input_grad, qkv_grad, out_grad = pl.pallas_call(
        kernel,
        out_shape=(
            jax.ShapeDtypeStruct((1, STEPS), F32),
            jax.ShapeDtypeStruct((STEPS, D), BF16),
            jax.ShapeDtypeStruct((16, 3 * D), F32),
            jax.ShapeDtypeStruct((16, D), F32),
        ),
        in_specs=[away, vmem, vmem, vmem, away, away, vmem, vmem, vmem, vmem],
        out_specs=(vmem, vmem, vmem, vmem),
        scratch_shapes=scratch,
        compiler_params=pltpu.CompilerParams(
            collective_id=0, has_side_effects=True, vmem_limit_bytes=60 * 2**20
        ),
    )(
        hidden[0, 0], done_step, rows, gain_t[None], w_qkv_t, w_out_t, gain_a[None], w_qkv_a,
        w_out_a, w_value[None],
    )
    values = values.reshape(-1, AGENTS).T
    return values[None], input_grad[None, None], qkv_grad, out_grad


def solution(mesh):
    in_specs = (
        P("env", "tm", None, None),
        P("env", "tm"),
        P("env", None, "tm"),
        P("env", None, "tm"),
        P(),
        P(),
        P(),
        P(),
        P("tm", None),
        P("tm", None),
        P(),
    )
    out_specs = (P("env", None, "tm"), P("env", "tm", None, None), P("tm", None), P("tm", None))
    return jax.shard_map(
        per_device, mesh=mesh, in_specs=in_specs, out_specs=out_specs, check_vma=False
    )
```

```python
import math

import jax
import jax.numpy as jnp
from jax import lax
from jax.experimental import pallas as pl
from jax.experimental.pallas import tpu as pltpu
from jax.sharding import PartitionSpec as P

F32, BF16 = jnp.float32, jnp.bfloat16
HEADS, D, STEPS, AGENTS = 8, 1024, 256, 64
HD = D // HEADS
SCALE = 1.0 / math.sqrt(HD)
NEG = -1e30
BAR, V2_AT, G2_AT = 5, 3, 7


def dot(a, b, ca, cb):
    return lax.dot_general(a, b, (((ca,), (cb,)), ((), ())), preferred_element_type=F32)


def nn(a, b):
    return dot(a, b, 1, 0)


def nt(a, b):
    return dot(a, b, 1, 1)


def tn(a, b):
    return dot(a, b, 0, 0)


def iota(shape, axis):
    return lax.broadcasted_iota(jnp.int32, shape, axis)


def split(x):
    high = x.astype(BF16)
    return high, (x - high.astype(F32)).astype(BF16)


def pick(condition):
    return jnp.where(condition, 1.0, 0.0).astype(BF16)


def step_to_block(flip):
    i, c = iota((256, 256), 1 if flip else 0), iota((256, 256), 0 if flip else 1)
    return pick(((i // 4) % 4 == c // 64) & (c % 64 == (i // 16) * 4 + i % 4))


def block_to_agent(flip):
    i, c = iota((256, 256), 1 if flip else 0), iota((256, 256), 0 if flip else 1)
    return pick((i % 16 == c // 16) & (i // 16 == c % 16))


def kernel(
    hidden_h, done_v, rows_v, gain_t_v, wqkv_h, wout_h, gain_a_v, wqkva_v, wouta_v, wval_v,
    values_o, igrad_o, qkvg_o, outg_o,
    hid, wqkv, wout, norm_t, qkv, prob_t, mixed, stage1, a1, r1, xr,
    w2, vb1, vb2, zb1, zb2, z128, na, nat, qk, prob_a, dqk, dqr, trow, gnorm, stage2, a2, r2, gh,
    tb, p1y, p1x, s1, s2, p2x, p2y, s3, pz, eb, us1, uz, um, uxy, uf, ue, up, uq, uw, ux,
    lsem, gs, gr, as1, ar1, as2, ar2, ss, sr, rs, rr,
):
    me, env = lax.axis_index("tm"), lax.axis_index("env")
    core, xl = env % 2, env // 2
    xh, z, y = me // 32, (me // 4) % 8, me % 4
    x_at = xh * 2 + xl
    core_id = {"env": env + 1 - 2 * core}

    def tm_at(xh_, z_, y_):
        return {"tm": xh_ * 32 + z_ * 4 + y_}

    def x_of(i):
        to = (x_at + i) % 4
        return to // 2, to % 2

    def x_peer(i):
        to_h, to_l = x_of(i)
        return {"env": to_l * 2 + core, "tm": to_h * 32 + z * 4 + y}

    def y_peer(i):
        return tm_at(xh, z, (y + i) % 4)

    def z_peer(i):
        return tm_at(xh, (z + i) % 8, y)

    def xy_of(i):
        to = (xh * 4 + y + i) % 8
        return to // 4, to % 4

    def xy_peer(i):
        to_h, to_y = xy_of(i)
        return tm_at(to_h, z, to_y)

    def send(src, dst, sems, k, where):
        copy = pltpu.make_async_remote_copy(
            src_ref=src, dst_ref=dst, send_sem=sems[0].at[k], recv_sem=sems[1].at[k],
            device_id=where, device_id_type=pl.DeviceIdType.MESH,
        )
        copy.start()
        return copy

    def spread(body):
        def step(i, carry):
            body(lax.rem(me + i, 64))
            return carry
        lax.fori_loop(1, 64, step, 0)

    barrier = pltpu.get_barrier_semaphore()

    def greet(where):
        pl.semaphore_signal(
            barrier, inc=1, device_id=where, device_id_type=pl.DeviceIdType.MESH
        )

    for i in range(1, 8):
        greet(z_peer(i))
    for i in range(1, 8):
        greet(xy_peer(i))
    greet({"env": (env + 2) % 4, "tm": (1 - xh) * 32 + z * 4 + y})
    for i in (1, 2, 3):
        greet({"env": (env + i) % 4})

    loads = [pltpu.make_async_copy(hidden_h, hid, lsem.at[0])]
    for j in range(6):
        at = (slice(None), slice(512 * j, 512 * j + 512))
        loads.append(pltpu.make_async_copy(wqkv_h.at[at], wqkv.at[at], lsem.at[1 + j]))
    loads.append(pltpu.make_async_copy(wout_h, wout, lsem.at[7]))
    for load in loads:
        load.start()

    w_value = wval_v[...]
    lane_off = (me % 8) * 16
    spot = iota((16, 128), 1) == iota((16, 128), 0) + lane_off
    own_line = iota((8, 128), 0) == me // 8

    def to_lanes(column):
        return jnp.sum(jnp.where(spot, column, 0.0), axis=0, keepdims=True)

    def rows_of(y_):
        return pl.ds(pl.multiple_of(y_ * 16, 16), 16)

    own_rows = rows_of(y)
    for half in range(2):
        at = pl.multiple_of(core * D + half * 512 + xl * 256, 256)
        w2[core, half, xl, xh, z, own_rows, :] = wqkva_v[:, pl.ds(at, 256)]
    v_part = jnp.sum(wouta_v[...].astype(F32) * w_value, axis=1, keepdims=True)
    vb1[0] = jnp.where(own_line, to_lanes(v_part), 0.0)

    G, S, R = (gs, gr), (ss, sr), (rs, rr)
    both, every = pl.ds(0, 2), pl.ds(0, 8)
    live = {}

    def begin(name, i, *what):
        live[(name, i)] = send(*what)

    def finish(name, n):
        for i in range(1, n + 1):
            live[(name, i)].wait()

    def g_z():
        ref = w2.at[core, both, xl, xh, z, own_rows]
        for i in range(1, 8):
            begin("gz", i, ref, ref, G, i - 1, z_peer(i))

    def g_2():
        finish("gz", 7)
        for i in (1, 2, 3):
            for half, peer, k in ((0, x_peer(i), 6), (1, y_peer(i), 9)):
                ref = w2.at[core, half, xl, xh, every, own_rows]
                begin(f"g2{half}", i, ref, ref, G, k + i, peer)

    def to_core(k, ref):
        begin("gc", k + 1, ref, ref, G, 19 + k, core_id)

    def g_3():
        finish("g20", 3)
        ref = w2.at[core, 0, both, both, every, own_rows]
        for i in (1, 2, 3):
            begin("g30", i, ref, ref, G, 12 + i, y_peer(i))
        to_core(0, ref)
        finish("g21", 3)
        ref = w2.at[core, 1, xl, xh]
        for i in (1, 2, 3):
            begin("g31", i, ref, ref, G, 15 + i, x_peer(i))
        to_core(1, ref)

    def g_end():
        for i in (1, 3, 2):
            live[("g30", i)].wait()
            to_core(1 + i, w2.at[core, 0, both, both, every, rows_of((y + 4 - i) % 4)])
            live[("g31", i)].wait()
            from_h, from_l = x_of(4 - i)
            to_core(4 + i, w2.at[core, 1, from_l, from_h])

    def v_1():
        for i in range(1, 8):
            begin("v1", i, vb1.at[0], vb1.at[i], S, i - 1, xy_peer(i))

    def v_2():
        finish("v1", 7)
        vb2[0] = jnp.sum(vb1[...], axis=0)
        for i in range(1, 8):
            begin("v2", i, vb2.at[0], vb2.at[i], S, 6 + i, z_peer(i))

    def z_1():
        finish("v2", 7)
        v8 = jnp.sum(vb2[...], axis=0)
        rows = []
        for h in range(HEADS):
            w_v = wqkva_v[:, 2 * D + h * HD : 2 * D + (h + 1) * HD].astype(F32)
            col = jnp.sum(w_v * v8[h : h + 1, :], axis=1, keepdims=True)
            rows.append(to_lanes(col))
        zb1[xh, y] = jnp.concatenate(rows, axis=0)
        for i in range(1, 8):
            begin("z1", i, zb1.at[xh, y], zb1.at[xh, y], S, 13 + i, xy_peer(i))

    def z_2():
        finish("z1", 7)
        zb2[z] = jnp.sum(zb1[...], axis=1)
        for i in range(1, 8):
            begin("z2", i, zb2.at[z], zb2.at[z], S, 20 + i, z_peer(i))

    def z_end():
        finish("z2", 7)
        tiles = []
        for i in range(2):
            for j in range(4):
                tiles.append(zb2[2 * j, i] + zb2[2 * j + 1, i])
        z_hi, z_lo = split(jnp.concatenate(tiles, axis=1))
        z128[...] = jnp.zeros((128, D), BF16)
        z128[0:16, :] = jnp.concatenate([z_hi, z_hi], axis=0)
        z128[16:32, :] = jnp.concatenate([z_lo, jnp.zeros_like(z_lo)], axis=0)

    loads[0].wait()
    x = hid[...].astype(F32)
    inv_t = lax.rsqrt(jnp.mean(x * x, axis=1, keepdims=True) + 1e-6)
    norm_t[...] = (x * inv_t * gain_t_v[...]).astype(BF16)
    for j in range(6):
        loads[1 + j].wait()
        at = slice(512 * j, 512 * j + 512)
        qkv[:, at] = nn(norm_t[...], wqkv[:, at]).astype(BF16)
        if j == BAR:
            pl.semaphore_wait(barrier, 18)
            g_z()
            v_1()
    done = done_v[...]
    ri, ci = iota((STEPS, STEPS), 0), iota((STEPS, STEPS), 1)
    allowed_t = (ri >= ci) & ((ri > done) == (ci > done))
    for h in range(HEADS):
        at = slice(h * HD, (h + 1) * HD)
        s = nt(qkv[:, at], qkv[:, D + h * HD : D + (h + 1) * HD]) * SCALE
        s = jnp.where(allowed_t, s, NEG)
        e = jnp.exp(s - jnp.max(s, axis=1, keepdims=True))
        p = (e / jnp.sum(e, axis=1, keepdims=True)).astype(BF16)
        prob_t[h] = p
        mixed[:, at] = nn(p, qkv[:, 2 * D + h * HD : 2 * D + (h + 1) * HD]).astype(BF16)
        if h == V2_AT:
            v_2()
        if h == G2_AT:
            g_2()
    loads[7].wait()
    turn = step_to_block(False)
    for q in range(4):
        at = slice(256 * q, 256 * q + 256)
        h1 = (hid[:, at].astype(F32) + nn(mixed[...], wout[:, at])).astype(BF16)
        for j in range(4):
            stage1[j, q * 64 : q * 64 + 64, :] = h1[j * 64 : j * 64 + 64, :]
    for j in range(4):
        a1[j * 256 : j * 256 + 256, :] = nn(turn, stage1[j]).astype(BF16)

    def block(peer):
        return pl.ds(pl.multiple_of(peer * 16, 16), 16)

    def put_1(peer):
        send(a1.at[block(peer)], r1.at[block(me)], (as1, ar1), 0, {"tm": peer})

    spread(put_1)
    r1[block(me), :] = a1[block(me), :]

    def wait_all(src, dst, sems):
        pltpu.make_async_remote_copy(
            src_ref=src.at[pl.ds(0, 1008)], dst_ref=dst.at[pl.ds(0, 1008)], send_sem=sems[0].at[0],
            recv_sem=sems[1].at[0], device_id=core_id, device_id_type=pl.DeviceIdType.MESH,
        ).wait()

    z_1()
    g_3()
    z_2()
    z_end()
    wait_all(a1, r1, (as1, ar1))

    unturn = block_to_agent(False)
    for j in range(4):
        got = nn(unturn, r1[j * 256 : j * 256 + 256, :]).astype(BF16)
        for q in range(4):
            for s in range(4):
                i = (q * 4 + s) * 16
                xr[s * 64 + j * 16 : s * 64 + j * 16 + 16, q * 256 : q * 256 + 256] = got[
                    i : i + 16, :
                ]
    xa = xr[...].astype(F32)
    inv_a = lax.rsqrt(jnp.mean(xa * xa, axis=1, keepdims=True) + 1e-6)
    h1_value = jnp.sum(xa * w_value, axis=1, keepdims=True)
    normed = xa * inv_a * gain_a_v[...]
    na[...] = normed.astype(BF16)
    for j in range(4):
        nat[0, j * 256 : j * 256 + 256, :] = normed[:, j * 256 : j * 256 + 256].T.astype(BF16)
    begin("nat", 1, nat.at[0], nat.at[1], G, 27, core_id)
    s_rows = nt(z128[0:32, :], na[...])
    s_rows = s_rows[0:8] + s_rows[16:24]
    diag = ri == ci
    alive_row, target_row = rows_v[0:1, :], rows_v[1:2, :]

    def to_column(row):
        return jnp.sum(jnp.where(diag, row, 0.0), axis=1, keepdims=True)

    alive_col, target_col = to_column(alive_row), to_column(target_row)
    g_end()

    def project(which):
        for half in range(2):
            for l in range(2):
                at = half * 512 + l * 256
                w = w2[which, half, l].reshape(D, 256)
                qk[which, :, at : at + 256] = nn(na[...], w).astype(BF16)

    project(core)
    finish("gc", 8)
    project(1 - core)
    square = iota((128, 128), 0), iota((128, 128), 1)
    same_step = (square[0] // 64) == (square[1] // 64)
    sums = []
    for p in range(2):
        rows = slice(128 * p, 128 * p + 128)
        seen = same_step & ((alive_row[:, rows] == 1.0) | (square[0] == square[1]))
        total = jnp.zeros((128, 1), F32)
        for h in range(HEADS):
            at = slice(h * HD, (h + 1) * HD)
            s = nt(qk[0, rows, at], qk[1, rows, at]) * SCALE
            s = jnp.where(seen, s, NEG)
            e = jnp.exp(s - jnp.max(s, axis=1, keepdims=True))
            e = e / jnp.sum(e, axis=1, keepdims=True)
            prob_a[h, p] = e
            total = total + jnp.sum(e * s_rows[h : h + 1, rows], axis=1, keepdims=True)
        sums.append(total)
    predicted = h1_value + jnp.concatenate(sums, axis=0)
    err = 32.0 * alive_col * (predicted - target_col)
    values_o[...] = jnp.sum(jnp.where(diag, predicted, 0.0), axis=0, keepdims=True)
    for p in range(2):
        rows = slice(128 * p, 128 * p + 128)
        for h in range(HEADS):
            at = slice(h * HD, (h + 1) * HD)
            e = prob_a[h, p]
            s_row = s_rows[h : h + 1, rows]
            pv = jnp.sum(e * s_row, axis=1, keepdims=True)
            weighted = e * err[rows, :]
            trow[h : h + 1, rows] = jnp.sum(weighted, axis=0, keepdims=True)
            ds = weighted * (s_row - pv) * SCALE
            dqk[0, rows, at] = nn(ds.astype(BF16), qk[1, rows, at]).astype(BF16)
            dqk[1, rows, at] = nn(ds.T.astype(BF16), qk[0, rows, at]).astype(BF16)
    begin("dqk", 1, dqk.at[1 - core], dqr, G, 28, core_id)

    t_hi = trow[...].astype(BF16).astype(F32)
    t_lo = trow[...] - t_hi
    u_all = nn(jnp.concatenate([t_hi, t_lo], axis=0).astype(BF16), na[...])
    u_all = u_all[0:8] + u_all[8:16]
    for i in range(8):
        for j in range(2):
            at = (j * 4 + i // 2) * 128
            us1[i, j] = u_all[:, at : at + 128]
    for i in range(1, 8):
        begin("uz", i, us1.at[(z + i) % 8], uz.at[i - 1], S, 27 + i, z_peer(i))

    live[("nat", 1)].wait()
    live[("dqk", 1)].wait()
    for half in range(2):
        for l in range(2):
            at = half * 512 + l * 256
            part = nn(nat[0], dqk[core, :, at : at + 256]) + nn(nat[1], dqr[:, at : at + 256])
            tb[half, l] = part.astype(BF16).reshape(2, 8, 64, 256)
        for i in (1, 2, 3):
            if half == 0:
                begin(
                    "p1y", i, tb.at[0, both, both, every, rows_of((y + i) % 4)], p1y.at[i - 1],
                    R, i - 1, y_peer(i),
                )
            else:
                to_h, to_l = x_of(i)
                begin("p1x", i, tb.at[1, to_l, to_h], p1x.at[i - 1], R, 2 + i, x_peer(i))

    t_all = jnp.concatenate([t_hi, t_lo, t_hi, jnp.zeros((104, STEPS), F32)], axis=0)
    t_col = t_all.T.astype(BF16)
    for i in range(4):
        at = slice(256 * i, 256 * i + 256)
        part = nn(t_col, z128[:, at])
        for c in range(2):
            for half in range(2):
                for l in range(2):
                    w = w2[c, half, l, i // 2, 4 * (i % 2) : 4 * (i % 2) + 4].reshape(256, 256)
                    lanes = half * 512 + l * 256
                    part = part + nt(dqk[c, :, lanes : lanes + 256], w)
        gnorm[:, at] = part * gain_a_v[:, at]
    gy = gnorm[...]
    xa = xr[...].astype(F32)
    pull = jnp.mean(xa * gy, axis=1, keepdims=True) * (inv_a * inv_a * inv_a)
    grad = (err * w_value + gy * inv_a - xa * pull).astype(BF16)
    turn = block_to_agent(True)
    for j in range(4):
        for q in range(4):
            for s in range(4):
                i = (q * 4 + s) * 16
                stage2[i : i + 16, j * 256 : j * 256 + 256] = grad[
                    s * 64 + j * 16 : s * 64 + j * 16 + 16, q * 256 : q * 256 + 256
                ]
    for j in range(4):
        a2[j * 256 : j * 256 + 256, :] = nn(turn, stage2[:, j * 256 : j * 256 + 256]).astype(BF16)

    def put_2(peer):
        send(a2.at[block(peer)], r2.at[block(me)], (as2, ar2), 0, {"tm": peer})

    spread(put_2)
    r2[block(me), :] = a2[block(me), :]

    def u_xy():
        finish("uz", 7)
        um[...] = us1[z] + jnp.sum(uz[...], axis=0)
        for i in range(1, 8):
            begin("uxy", i, um.at[xy_of(i)[0]], uxy.at[i - 1], S, 34 + i, xy_peer(i))

    def u_env():
        finish("uxy", 7)
        uf[...] = um[xh] + jnp.sum(uxy[...], axis=0)
        for i in (1, 2, 3):
            begin("ue", i, uf, ue.at[i - 1], S, 41 + i, {"env": (env + i) % 4})

    def u_mix():
        finish("ue", 3)
        u = uf[...] + jnp.sum(ue[...], axis=0)
        v8 = jnp.sum(vb2[...], axis=0)
        lines = []
        for h in range(HEADS):
            at = slice(2 * D + h * HD, 2 * D + (h + 1) * HD)
            col = jnp.sum(jnp.where(spot, u[h : h + 1, :], 0.0), axis=1, keepdims=True)
            qkvg_o[:, at] = col * v8[h : h + 1, :]
            lines.append(jnp.sum(col * wqkva_v[:, at].astype(F32), axis=0, keepdims=True))
        up[...] = jnp.concatenate(lines, axis=0)
        for i in range(1, 8):
            begin("uq", i, up, uq.at[i - 1], S, 44 + i, z_peer(i))

    def u_last():
        finish("uq", 7)
        uw[...] = up[...] + jnp.sum(uq[...], axis=0)
        for i in range(1, 8):
            begin("ux", i, uw, ux.at[i - 1], S, 51 + i, xy_peer(i))

    def u_end():
        finish("ux", 7)
        total = uw[...] + jnp.sum(ux[...], axis=0)
        row = jnp.sum(jnp.where(own_line, total, 0.0), axis=0, keepdims=True)
        outg_o[...] = jnp.sum(jnp.where(spot, row, 0.0), axis=1, keepdims=True) * w_value

    def r_2():
        finish("p1y", 3)
        for l in range(2):
            for i in range(2):
                total = tb[0, l, i, :, own_rows, :].astype(F32)
                for k in range(3):
                    total = total + p1y[k, l, i].astype(F32)
                s1[l, i] = total.astype(BF16)
        for i in (1, 2, 3):
            to_h, to_l = x_of(i)
            begin("p2x", i, s1.at[to_l, to_h], p2x.at[i - 1], R, 5 + i, x_peer(i))
        finish("p1x", 3)
        for i in range(8):
            total = tb[1, xl, xh, i].astype(F32)
            for k in range(3):
                total = total + p1x[k, i].astype(F32)
            s2[i] = total.astype(BF16)
        for i in (1, 2, 3):
            begin(
                "p2y", i, s2.at[every, rows_of((y + i) % 4)], p2y.at[i - 1], R, 8 + i, y_peer(i)
            )

    def r_z():
        finish("p2x", 3)
        total = s1[xl, xh].astype(F32)
        for k in range(3):
            total = total + p2x[k].astype(F32)
        s3[0] = total.astype(BF16)
        finish("p2y", 3)
        total = s2[:, own_rows, :].astype(F32)
        for k in range(3):
            total = total + p2y[k].astype(F32)
        s3[1] = total.astype(BF16)
        for i in range(1, 8):
            begin("pz", i, s3.at[both, (z + i) % 8], pz.at[i - 1], R, 11 + i, z_peer(i))

    def r_env():
        finish("pz", 7)
        total = s3[:, z].astype(F32)
        for k in range(7):
            total = total + pz[k].astype(F32)
        eb[env] = total
        for i in (1, 2, 3):
            begin("eb", i, eb.at[env], eb.at[env], R, 18 + i, {"env": (env + i) % 4})

    def r_end():
        finish("eb", 3)
        for e in range(4):
            for half in range(2):
                at = (e % 2) * D + half * 512 + (e // 2) * 256
                qkvg_o[:, at : at + 256] = eb[e, half]

    u_xy()
    u_env()

    wait_all(a2, r2, (as2, ar2))
    unturn = step_to_block(True)
    for j in range(4):
        got = nn(unturn, r2[j * 256 : j * 256 + 256, :]).astype(BF16)
        for q in range(4):
            gh[j * 64 : j * 64 + 64, q * 256 : q * 256 + 256] = got[q * 64 : q * 64 + 64, :]
    u_mix()
    after = {0: r_2, 3: u_last, 7: r_z}
    for h in range(HEADS):
        at = slice(h * HD, (h + 1) * HD)
        at_k, at_v = slice(D + h * HD, D + (h + 1) * HD), slice(2 * D + h * HD, 2 * D + (h + 1) * HD)
        gm = nt(gh[...], wout[at, :]).astype(BF16)
        p = prob_t[h]
        pf = p.astype(F32)
        dp = nt(gm, qkv[:, at_v])
        ds = (pf * (dp - jnp.sum(pf * dp, axis=1, keepdims=True)) * SCALE)
        q_h, k_h = qkv[:, at], qkv[:, at_k]
        qkv[:, at_v] = nn(pf.T.astype(BF16), gm).astype(BF16)
        qkv[:, at] = nn(ds.astype(BF16), k_h).astype(BF16)
        qkv[:, at_k] = nn(ds.T.astype(BF16), q_h).astype(BF16)
        if h in after:
            after[h]()
    for i in range(4):
        at = slice(256 * i, 256 * i + 256)
        gnorm[:, at] = nt(qkv[...], wqkv[at, :]) * gain_t_v[:, at]
    gy = gnorm[...]
    x = hid[...].astype(F32)
    inv_t = lax.rsqrt(jnp.mean(x * x, axis=1, keepdims=True) + 1e-6)
    pull = jnp.mean(x * gy, axis=1, keepdims=True) * (inv_t * inv_t * inv_t)
    igrad_o[...] = (gh[...].astype(F32) + gy * inv_t - x * pull).astype(BF16)
    u_end()
    r_env()
    r_end()


def per_device(
    hidden, done_step, alive, targets, gain_t, w_qkv_t, w_out_t, gain_a, w_qkv_a, w_out_a, w_value
):
    rows = jnp.stack([alive[0].astype(F32).T.reshape(-1), targets[0].T.reshape(-1)])
    vmem = pl.BlockSpec(memory_space=pltpu.VMEM)
    away = pl.BlockSpec(memory_space=pl.ANY)
    mem = pltpu.VMEM
    dma = pltpu.SemaphoreType.DMA
    tile = (8, 128)
    scratch = [
        mem((STEPS, D), BF16), mem((D, 3 * D), BF16), mem((D, D), BF16), mem((STEPS, D), BF16),
        mem((STEPS, 3 * D), BF16), mem((HEADS, STEPS, STEPS), BF16), mem((STEPS, D), BF16),
        mem((4, 256, 256), BF16), mem((1024, 256), BF16), mem((1024, 256), BF16),
        mem((STEPS, D), BF16),
        mem((2, 2, 2, 2, 8, 64, 256), BF16), mem((8, *tile), F32), mem((8, *tile), F32),
        mem((2, 4, *tile), F32), mem((8, 2, *tile), F32), mem((128, D), BF16),
        mem((STEPS, D), BF16), mem((2, D, STEPS), BF16), mem((2, STEPS, D), BF16),
        mem((HEADS, 2, 128, 128), F32), mem((2, STEPS, D), BF16), mem((STEPS, D), BF16),
        mem((HEADS, STEPS), F32), mem((STEPS, D), F32), mem((256, 1024), BF16),
        mem((1024, 256), BF16), mem((1024, 256), BF16), mem((STEPS, D), BF16),
        mem((2, 2, 2, 8, 64, 256), BF16), mem((3, 2, 2, 8, 16, 256), BF16),
        mem((3, 8, 64, 256), BF16), mem((2, 2, 8, 16, 256), BF16), mem((8, 64, 256), BF16),
        mem((3, 8, 16, 256), BF16), mem((3, 8, 16, 256), BF16), mem((2, 8, 16, 256), BF16),
        mem((7, 2, 16, 256), BF16), mem((4, 2, 16, 256), F32),
        mem((8, 2, *tile), F32), mem((7, 2, *tile), F32), mem((2, *tile), F32),
        mem((7, *tile), F32), mem(tile, F32), mem((3, *tile), F32), mem(tile, F32),
        mem((7, *tile), F32), mem(tile, F32), mem((7, *tile), F32),
        dma((8,)), dma((29,)), dma((29,)), dma((1,)), dma((1,)), dma((1,)), dma((1,)),
        dma((59,)), dma((59,)), dma((22,)), dma((22,)),
    ]
    values, input_grad, qkv_grad, out_grad = pl.pallas_call(
        kernel,
        out_shape=(
            jax.ShapeDtypeStruct((1, STEPS), F32),
            jax.ShapeDtypeStruct((STEPS, D), BF16),
            jax.ShapeDtypeStruct((16, 3 * D), F32),
            jax.ShapeDtypeStruct((16, D), F32),
        ),
        in_specs=[away, vmem, vmem, vmem, away, away, vmem, vmem, vmem, vmem],
        out_specs=(vmem, vmem, vmem, vmem),
        scratch_shapes=scratch,
        compiler_params=pltpu.CompilerParams(
            collective_id=0, has_side_effects=True, vmem_limit_bytes=60 * 2**20
        ),
    )(
        hidden[0, 0], done_step, rows, gain_t[None], w_qkv_t, w_out_t, gain_a[None], w_qkv_a,
        w_out_a, w_value[None],
    )
    values = values.reshape(-1, AGENTS).T
    return values[None], input_grad[None, None], qkv_grad, out_grad


def solution(mesh):
    in_specs = (
        P("env", "tm", None, None),
        P("env", "tm"),
        P("env", None, "tm"),
        P("env", None, "tm"),
        P(),
        P(),
        P(),
        P(),
        P("tm", None),
        P("tm", None),
        P(),
    )
    out_specs = (P("env", None, "tm"), P("env", "tm", None, None), P("tm", None), P("tm", None))
    return jax.shard_map(
        per_device, mesh=mesh, in_specs=in_specs, out_specs=out_specs, check_vma=False
    )
```

```python
import math

import jax
import jax.numpy as jnp
from jax import lax
from jax.experimental import pallas as pl
from jax.experimental.pallas import tpu as pltpu
from jax.sharding import PartitionSpec as P

F32, BF16 = jnp.float32, jnp.bfloat16
HEADS, D, STEPS, AGENTS = 8, 1024, 256, 64
HD = D // HEADS
SCALE = 1.0 / math.sqrt(HD)
NEG = -1e30
BAR, V2_AT, G2_AT = 5, 3, 7


def dot(a, b, ca, cb):
    return lax.dot_general(a, b, (((ca,), (cb,)), ((), ())), preferred_element_type=F32)


def nn(a, b):
    return dot(a, b, 1, 0)


def nt(a, b):
    return dot(a, b, 1, 1)


def tn(a, b):
    return dot(a, b, 0, 0)


def iota(shape, axis):
    return lax.broadcasted_iota(jnp.int32, shape, axis)


def split(x):
    high = x.astype(BF16)
    return high, (x - high.astype(F32)).astype(BF16)


def pick(condition):
    return jnp.where(condition, 1.0, 0.0).astype(BF16)


def step_to_block(flip):
    i, c = iota((256, 256), 1 if flip else 0), iota((256, 256), 0 if flip else 1)
    return pick(((i // 4) % 4 == c // 64) & (c % 64 == (i // 16) * 4 + i % 4))


def block_to_agent(flip):
    i, c = iota((256, 256), 1 if flip else 0), iota((256, 256), 0 if flip else 1)
    return pick((i % 16 == c // 16) & (i // 16 == c % 16))


def kernel(
    hidden_h, done_v, alive_v, target_v, gain_t_v, wqkv_h, wout_h, gain_a_v, wqkva_v, wouta_v, wval_v,
    values_o, igrad_o, qkvg_o, outg_o,
    hid, wqkv, wout, norm_t, qkv, prob_t, mixed, stage1, a1, r1, xr,
    w2, vb1, vb2, zb1, zb2, z128, na, nat, qk, prob_a, dqk, dqr, trow, gnorm, stage2, a2, r2, gh,
    tb, opp_y, opp_x, p1y, p1x, s1, s2, p2x, p2y, s3, pz, eb, us1, uz, um, uxy, uf, ue, up, uq, uw, ux,
    lsem, gs, gr, as1, ar1, as2, ar2, ss, sr, rs, rr,
):
    me, env = lax.axis_index("tm"), lax.axis_index("env")
    core, xl = env % 2, env // 2
    xh, z, y = me // 32, (me // 4) % 8, me % 4
    x_at = xh * 2 + xl
    core_id = {"env": env + 1 - 2 * core}

    def tm_at(xh_, z_, y_):
        return {"tm": xh_ * 32 + z_ * 4 + y_}

    def x_of(i):
        to = (x_at + i) % 4
        return to // 2, to % 2

    def x_peer(i):
        to_h, to_l = x_of(i)
        return {"env": to_l * 2 + core, "tm": to_h * 32 + z * 4 + y}

    def y_peer(i):
        return tm_at(xh, z, (y + i) % 4)

    def z_peer(i):
        return tm_at(xh, (z + i) % 8, y)

    def xy_of(i):
        to = (xh * 4 + y + i) % 8
        return to // 4, to % 4

    def xy_peer(i):
        to_h, to_y = xy_of(i)
        return tm_at(to_h, z, to_y)

    def send(src, dst, sems, k, where):
        copy = pltpu.make_async_remote_copy(
            src_ref=src, dst_ref=dst, send_sem=sems[0].at[k], recv_sem=sems[1].at[k],
            device_id=where, device_id_type=pl.DeviceIdType.MESH,
        )
        copy.start()
        return copy

    def spread(body):
        def step(i, carry):
            body(lax.rem(me + i, 64))
            return carry
        lax.fori_loop(1, 64, step, 0)

    barrier = pltpu.get_barrier_semaphore()

    def greet(where):
        pl.semaphore_signal(
            barrier, inc=1, device_id=where, device_id_type=pl.DeviceIdType.MESH
        )

    for i in range(1, 8):
        greet(z_peer(i))
    for i in range(1, 8):
        greet(xy_peer(i))
    greet({"env": (env + 2) % 4, "tm": (1 - xh) * 32 + z * 4 + y})
    for i in (1, 2, 3):
        greet({"env": (env + i) % 4})

    loads = [pltpu.make_async_copy(hidden_h, hid, lsem.at[0])]
    for j in range(6):
        at = (slice(None), slice(512 * j, 512 * j + 512))
        loads.append(pltpu.make_async_copy(wqkv_h.at[at], wqkv.at[at], lsem.at[1 + j]))
    loads.append(pltpu.make_async_copy(wout_h, wout, lsem.at[7]))
    for load in loads:
        load.start()

    w_value = wval_v[...]
    lane_off = (me % 8) * 16
    spot = iota((16, 128), 1) == iota((16, 128), 0) + lane_off
    own_line = iota((8, 128), 0) == me // 8

    def to_lanes(column):
        return jnp.sum(jnp.where(spot, column, 0.0), axis=0, keepdims=True)

    def rows_of(y_):
        return pl.ds(pl.multiple_of(y_ * 16, 16), 16)

    own_rows = rows_of(y)
    for half in range(2):
        at = pl.multiple_of(core * D + half * 512 + xl * 256, 256)
        w2[core, half, xl, xh, z, own_rows, :] = wqkva_v[:, pl.ds(at, 256)]
    v_part = jnp.sum(wouta_v[...].astype(F32) * w_value, axis=1, keepdims=True)
    vb1[0] = jnp.where(own_line, to_lanes(v_part), 0.0)

    G, S, R = (gs, gr), (ss, sr), (rs, rr)
    both, every = pl.ds(0, 2), pl.ds(0, 8)
    live = {}

    def begin(name, i, *what):
        live[(name, i)] = send(*what)

    def finish(name, n):
        for i in range(1, n + 1):
            live[(name, i)].wait()

    def g_z():
        ref = w2.at[core, both, xl, xh, z, own_rows]
        for i in range(1, 8):
            begin("gz", i, ref, ref, G, i - 1, z_peer(i))

    def g_2():
        finish("gz", 7)
        for i in (1, 2, 3):
            for half, peer, k in ((0, x_peer(i), 6), (1, y_peer(i), 9)):
                ref = w2.at[core, half, xl, xh, every, own_rows]
                begin(f"g2{half}", i, ref, ref, G, k + i, peer)

    def to_core(k, ref):
        begin("gc", k + 1, ref, ref, G, 21 + k, core_id)

    first, second = pl.ds(0, 4), pl.ds(4, 4)

    def y_piece(i, zs_=every):
        return w2.at[core, 0, both, both, zs_, rows_of((y + i) % 4)]

    def x_piece(i, zs_=every):
        to_h, to_l = x_of(i)
        return w2.at[core, 1, to_l, to_h, zs_]

    def g_3():
        for half, part, peer in ((0, y_piece, y_peer), (1, x_piece, x_peer)):
            finish(f"g2{half}", 3)
            for i in (1, 3):
                begin(f"g3{half}", i, part(0), part(0), G, 13 + 4 * half + i // 2, peer(i))
            to_core(4 * half, part(0))

    def g_mid():
        for half, part, peer in ((0, y_piece, y_peer), (1, x_piece, x_peer)):
            for i, zs_ in ((1, first), (3, second)):
                live[(f"g3{half}", i)].wait()
                ref = part(4 - i, zs_)
                begin(f"g4{half}", i, ref, ref, G, 15 + 4 * half + i // 2, peer(i))
        for half, part in ((0, y_piece), (1, x_piece)):
            for i in (1, 3):
                to_core(4 * half + 1 + i // 2, part(4 - i))

    def g_end():
        for half, part in ((0, y_piece), (1, x_piece)):
            for i in (1, 3):
                live[(f"g4{half}", i)].wait()
            to_core(4 * half + 3, part(2))

    def v_1():
        for i in range(1, 8):
            begin("v1", i, vb1.at[0], vb1.at[i], S, i - 1, xy_peer(i))

    def v_2():
        finish("v1", 7)
        vb2[0] = jnp.sum(vb1[...], axis=0)
        for i in range(1, 8):
            begin("v2", i, vb2.at[0], vb2.at[i], S, 6 + i, z_peer(i))

    def z_1():
        finish("v2", 7)
        v8 = jnp.sum(vb2[...], axis=0)
        rows = []
        for h in range(HEADS):
            w_v = wqkva_v[:, 2 * D + h * HD : 2 * D + (h + 1) * HD].astype(F32)
            col = jnp.sum(w_v * v8[h : h + 1, :], axis=1, keepdims=True)
            rows.append(to_lanes(col))
        zb1[xh, y] = jnp.concatenate(rows, axis=0)
        for i in range(1, 8):
            begin("z1", i, zb1.at[xh, y], zb1.at[xh, y], S, 13 + i, xy_peer(i))

    def z_2():
        finish("z1", 7)
        zb2[z] = jnp.sum(zb1[...], axis=1)
        for i in range(1, 8):
            begin("z2", i, zb2.at[z], zb2.at[z], S, 20 + i, z_peer(i))

    def z_end():
        finish("z2", 7)
        tiles = []
        for i in range(2):
            for j in range(4):
                tiles.append(zb2[2 * j, i] + zb2[2 * j + 1, i])
        z_hi, z_lo = split(jnp.concatenate(tiles, axis=1))
        z128[...] = jnp.zeros((128, D), BF16)
        z128[0:16, :] = jnp.concatenate([z_hi, z_hi], axis=0)
        z128[16:32, :] = jnp.concatenate([z_lo, jnp.zeros_like(z_lo)], axis=0)

    loads[0].wait()
    x = hid[...].astype(F32)
    inv_t = lax.rsqrt(jnp.mean(x * x, axis=1, keepdims=True) + 1e-6)
    norm_t[...] = (x * inv_t * gain_t_v[...]).astype(BF16)
    for j in range(6):
        loads[1 + j].wait()
        at = slice(512 * j, 512 * j + 512)
        qkv[:, at] = nn(norm_t[...], wqkv[:, at]).astype(BF16)
        if j == BAR:
            pl.semaphore_wait(barrier, 18)
            g_z()
            v_1()
    done = done_v[...]
    ri, ci = iota((STEPS, STEPS), 0), iota((STEPS, STEPS), 1)
    allowed_t = (ri >= ci) & ((ri > done) == (ci > done))
    for h in range(HEADS):
        at = slice(h * HD, (h + 1) * HD)
        s = nt(qkv[:, at], qkv[:, D + h * HD : D + (h + 1) * HD]) * SCALE
        s = jnp.where(allowed_t, s, NEG)
        e = jnp.exp(s - jnp.max(s, axis=1, keepdims=True))
        p = (e / jnp.sum(e, axis=1, keepdims=True)).astype(BF16)
        prob_t[h] = p
        mixed[:, at] = nn(p, qkv[:, 2 * D + h * HD : 2 * D + (h + 1) * HD]).astype(BF16)
        if h == V2_AT:
            v_2()
        if h == G2_AT:
            g_2()
    loads[7].wait()
    turn = step_to_block(False)
    for q in range(4):
        at = slice(256 * q, 256 * q + 256)
        h1 = (hid[:, at].astype(F32) + nn(mixed[...], wout[:, at])).astype(BF16)
        for j in range(4):
            stage1[j, q * 64 : q * 64 + 64, :] = h1[j * 64 : j * 64 + 64, :]
    for j in range(4):
        a1[j * 256 : j * 256 + 256, :] = nn(turn, stage1[j]).astype(BF16)

    def block(peer):
        return pl.ds(pl.multiple_of(peer * 16, 16), 16)

    def put_1(peer):
        send(a1.at[block(peer)], r1.at[block(me)], (as1, ar1), 0, {"tm": peer})

    spread(put_1)
    r1[block(me), :] = a1[block(me), :]

    def wait_all(src, dst, sems):
        pltpu.make_async_remote_copy(
            src_ref=src.at[pl.ds(0, 1008)], dst_ref=dst.at[pl.ds(0, 1008)], send_sem=sems[0].at[0],
            recv_sem=sems[1].at[0], device_id=core_id, device_id_type=pl.DeviceIdType.MESH,
        ).wait()

    z_1()
    g_3()
    z_2()
    g_mid()
    z_end()
    wait_all(a1, r1, (as1, ar1))

    unturn = block_to_agent(False)
    for j in range(4):
        got = nn(unturn, r1[j * 256 : j * 256 + 256, :]).astype(BF16)
        for q in range(4):
            for s in range(4):
                i = (q * 4 + s) * 16
                xr[s * 64 + j * 16 : s * 64 + j * 16 + 16, q * 256 : q * 256 + 256] = got[
                    i : i + 16, :
                ]
    xa = xr[...].astype(F32)
    inv_a = lax.rsqrt(jnp.mean(xa * xa, axis=1, keepdims=True) + 1e-6)
    h1_value = jnp.sum(xa * w_value, axis=1, keepdims=True)
    normed = xa * inv_a * gain_a_v[...]
    na[...] = normed.astype(BF16)
    for j in range(4):
        nat[0, j * 256 : j * 256 + 256, :] = normed[:, j * 256 : j * 256 + 256].T.astype(BF16)
    begin("nat", 1, nat.at[0], nat.at[1], G, 29, core_id)
    s_rows = nt(z128[0:32, :], na[...])
    s_rows = s_rows[0:8] + s_rows[16:24]
    diag = ri == ci
    alive_f, target_f = alive_v[...].astype(F32), target_v[...]

    def one_row(table):
        return jnp.concatenate([table[s : s + 1, :] for s in range(4)], axis=1)

    def to_column(row):
        return jnp.sum(jnp.where(diag, row, 0.0), axis=1, keepdims=True)

    alive_row = one_row(alive_f)
    alive_col, target_col = to_column(alive_row), to_column(one_row(target_f))
    g_end()

    def project(which):
        for half in range(2):
            for l in range(2):
                at = half * 512 + l * 256
                w = w2[which, half, l].reshape(D, 256)
                qk[which, :, at : at + 256] = nn(na[...], w).astype(BF16)

    project(core)
    finish("gc", 8)
    project(1 - core)
    square = iota((128, 128), 0), iota((128, 128), 1)
    same_step = (square[0] // 64) == (square[1] // 64)
    sums = []
    for p in range(2):
        rows = slice(128 * p, 128 * p + 128)
        seen = same_step & ((alive_row[:, rows] == 1.0) | (square[0] == square[1]))
        total = jnp.zeros((128, 1), F32)
        for h in range(HEADS):
            at = slice(h * HD, (h + 1) * HD)
            s = nt(qk[0, rows, at], qk[1, rows, at]) * SCALE
            s = jnp.where(seen, s, NEG)
            e = jnp.exp(s - jnp.max(s, axis=1, keepdims=True))
            e = e / jnp.sum(e, axis=1, keepdims=True)
            prob_a[h, p] = e
            total = total + jnp.sum(e * s_rows[h : h + 1, rows], axis=1, keepdims=True)
        sums.append(total)
    predicted = h1_value + jnp.concatenate(sums, axis=0)
    err = 32.0 * alive_col * (predicted - target_col)
    line = jnp.sum(jnp.where(diag, predicted, 0.0), axis=0, keepdims=True)
    for s in range(4):
        values_o[s : s + 1, :] = line[:, s * 64 : s * 64 + 64]
    for p in range(2):
        rows = slice(128 * p, 128 * p + 128)
        for h in range(HEADS):
            at = slice(h * HD, (h + 1) * HD)
            e = prob_a[h, p]
            s_row = s_rows[h : h + 1, rows]
            pv = jnp.sum(e * s_row, axis=1, keepdims=True)
            weighted = e * err[rows, :]
            trow[h : h + 1, rows] = jnp.sum(weighted, axis=0, keepdims=True)
            ds = weighted * (s_row - pv) * SCALE
            dqk[0, rows, at] = nn(ds.astype(BF16), qk[1, rows, at]).astype(BF16)
            dqk[1, rows, at] = nn(ds.T.astype(BF16), qk[0, rows, at]).astype(BF16)
    begin("dqk", 1, dqk.at[1 - core], dqr, G, 30, core_id)

    t_hi = trow[...].astype(BF16).astype(F32)
    t_lo = trow[...] - t_hi
    u_all = nn(jnp.concatenate([t_hi, t_lo], axis=0).astype(BF16), na[...])
    u_all = u_all[0:8] + u_all[8:16]
    for i in range(8):
        for j in range(2):
            at = (j * 4 + i // 2) * 128
            us1[i, j] = u_all[:, at : at + 128]
    for i in range(1, 8):
        begin("uz", i, us1.at[(z + i) % 8], uz.at[i - 1], S, 27 + i, z_peer(i))

    t_all = jnp.concatenate([t_hi, t_lo, t_hi, jnp.zeros((104, STEPS), F32)], axis=0)
    t_col = t_all.T.astype(BF16)
    for i in range(4):
        at = slice(256 * i, 256 * i + 256)
        part = nn(t_col, z128[:, at])
        for c in range(2):
            for half in range(2):
                for l in range(2):
                    w = w2[c, half, l, i // 2, 4 * (i % 2) : 4 * (i % 2) + 4].reshape(256, 256)
                    lanes = half * 512 + l * 256
                    part = part + nt(dqk[c, :, lanes : lanes + 256], w)
        gnorm[:, at] = part * gain_a_v[:, at]

    peers, opp = (y_peer, x_peer), (opp_y, opp_x)

    def term(half, i, zs_):
        if half == 0:
            return tb.at[0, both, both, zs_, rows_of((y + i) % 4)]
        to_h, to_l = x_of(i)
        return tb.at[1, to_l, to_h, zs_]

    def got_1(half, n, zs_):
        return p1y.at[n, both, both, zs_] if half == 0 else p1x.at[n, zs_]

    live[("nat", 1)].wait()
    live[("dqk", 1)].wait()
    for half in range(2):
        for l in range(2):
            at = half * 512 + l * 256
            part = nn(nat[0], dqk[core, :, at : at + 256]) + nn(nat[1], dqr[:, at : at + 256])
            tb[half, l] = part.astype(BF16).reshape(2, 8, 64, 256)
        for n, (i, across, plain) in enumerate(((1, first, second), (3, second, first))):
            begin(
                f"q{half}", i, term(half, 2, across), opp[half].at[n], R, 6 * half + n, peers[half](i)
            )
            begin(
                f"p{half}", i, term(half, i, plain), got_1(half, n, plain),
                R, 6 * half + 2 + n, peers[half](i),
            )

    gy = gnorm[...]
    xa = xr[...].astype(F32)
    pull = jnp.mean(xa * gy, axis=1, keepdims=True) * (inv_a * inv_a * inv_a)
    grad = (err * w_value + gy * inv_a - xa * pull).astype(BF16)
    turn = block_to_agent(True)
    for j in range(4):
        for q in range(4):
            for s in range(4):
                i = (q * 4 + s) * 16
                stage2[i : i + 16, j * 256 : j * 256 + 256] = grad[
                    s * 64 + j * 16 : s * 64 + j * 16 + 16, q * 256 : q * 256 + 256
                ]
    for j in range(4):
        a2[j * 256 : j * 256 + 256, :] = nn(turn, stage2[:, j * 256 : j * 256 + 256]).astype(BF16)

    def put_2(peer):
        send(a2.at[block(peer)], r2.at[block(me)], (as2, ar2), 0, {"tm": peer})

    spread(put_2)
    r2[block(me), :] = a2[block(me), :]

    def u_xy():
        finish("uz", 7)
        um[...] = us1[z] + jnp.sum(uz[...], axis=0)
        for i in range(1, 8):
            begin("uxy", i, um.at[xy_of(i)[0]], uxy.at[i - 1], S, 34 + i, xy_peer(i))

    def u_env():
        finish("uxy", 7)
        uf[...] = um[xh] + jnp.sum(uxy[...], axis=0)
        for i in (1, 2, 3):
            begin("ue", i, uf, ue.at[i - 1], S, 41 + i, {"env": (env + i) % 4})

    def u_mix():
        finish("ue", 3)
        u = uf[...] + jnp.sum(ue[...], axis=0)
        v8 = jnp.sum(vb2[...], axis=0)
        lines = []
        for h in range(HEADS):
            at = slice(2 * D + h * HD, 2 * D + (h + 1) * HD)
            col = jnp.sum(jnp.where(spot, u[h : h + 1, :], 0.0), axis=1, keepdims=True)
            qkvg_o[:, at] = col * v8[h : h + 1, :]
            lines.append(jnp.sum(col * wqkva_v[:, at].astype(F32), axis=0, keepdims=True))
        up[...] = jnp.concatenate(lines, axis=0)
        for i in range(1, 8):
            begin("uq", i, up, uq.at[i - 1], S, 44 + i, z_peer(i))

    def u_last():
        finish("uq", 7)
        uw[...] = up[...] + jnp.sum(uq[...], axis=0)
        for i in range(1, 8):
            begin("ux", i, uw, ux.at[i - 1], S, 51 + i, xy_peer(i))

    def u_end():
        finish("ux", 7)
        total = uw[...] + jnp.sum(ux[...], axis=0)
        row = jnp.sum(jnp.where(own_line, total, 0.0), axis=0, keepdims=True)
        outg_o[...] = jnp.sum(jnp.where(spot, row, 0.0), axis=1, keepdims=True) * w_value

    def r_1():
        for half in range(2):
            for n, (i, across) in enumerate(((1, first), (3, second))):
                live[(f"q{half}", i)].wait()
                z0 = 4 * n
                if half == 0:
                    rows = rows_of((y + i) % 4)
                    for l in range(2):
                        for k in range(2):
                            both_terms = tb[0, l, k, z0 : z0 + 4, rows, :] + opp_y[n, l, k]
                            tb[0, l, k, z0 : z0 + 4, rows, :] = both_terms
                else:
                    to_h, to_l = x_of(i)
                    for k in range(4):
                        tb[1, to_l, to_h, z0 + k] = tb[1, to_l, to_h, z0 + k] + opp_x[n, k]
                begin(
                    f"r{half}", i, term(half, i, across), got_1(half, n, across),
                    R, 6 * half + 4 + n, peers[half](i),
                )

    def r_2():
        for name in ("p0", "r0"):
            for i in (1, 3):
                live[(name, i)].wait()
        for l in range(2):
            for i in range(2):
                total = tb[0, l, i, :, own_rows, :].astype(F32)
                for k in range(2):
                    total = total + p1y[k, l, i].astype(F32)
                s1[l, i] = total.astype(BF16)
        for i in (1, 2, 3):
            to_h, to_l = x_of(i)
            begin("p2x", i, s1.at[to_l, to_h], p2x.at[i - 1], R, 11 + i, x_peer(i))
        for name in ("p1", "r1"):
            for i in (1, 3):
                live[(name, i)].wait()
        for i in range(8):
            total = tb[1, xl, xh, i].astype(F32)
            for k in range(2):
                total = total + p1x[k, i].astype(F32)
            s2[i] = total.astype(BF16)
        for i in (1, 2, 3):
            begin(
                "p2y", i, s2.at[every, rows_of((y + i) % 4)], p2y.at[i - 1], R, 14 + i, y_peer(i)
            )

    def r_z():
        finish("p2x", 3)
        total = s1[xl, xh].astype(F32)
        for k in range(3):
            total = total + p2x[k].astype(F32)
        s3[0] = total.astype(BF16)
        finish("p2y", 3)
        total = s2[:, own_rows, :].astype(F32)
        for k in range(3):
            total = total + p2y[k].astype(F32)
        s3[1] = total.astype(BF16)
        for i in range(1, 8):
            begin("pz", i, s3.at[both, (z + i) % 8], pz.at[i - 1], R, 17 + i, z_peer(i))

    def r_env():
        finish("pz", 7)
        total = s3[:, z].astype(F32)
        for k in range(7):
            total = total + pz[k].astype(F32)
        eb[env] = total
        for i in (1, 2, 3):
            begin("eb", i, eb.at[env], eb.at[env], R, 24 + i, {"env": (env + i) % 4})

    def r_end():
        finish("eb", 3)
        for e in range(4):
            for half in range(2):
                at = (e % 2) * D + half * 512 + (e // 2) * 256
                qkvg_o[:, at : at + 256] = eb[e, half]

    r_1()
    u_xy()
    r_2()
    u_env()

    wait_all(a2, r2, (as2, ar2))
    unturn = step_to_block(True)
    for j in range(4):
        got = nn(unturn, r2[j * 256 : j * 256 + 256, :]).astype(BF16)
        for q in range(4):
            gh[j * 64 : j * 64 + 64, q * 256 : q * 256 + 256] = got[q * 64 : q * 64 + 64, :]
    after = {1: r_z, 2: u_mix, 5: u_last}
    for h in range(HEADS):
        at = slice(h * HD, (h + 1) * HD)
        at_k, at_v = slice(D + h * HD, D + (h + 1) * HD), slice(2 * D + h * HD, 2 * D + (h + 1) * HD)
        gm = nt(gh[...], wout[at, :]).astype(BF16)
        p = prob_t[h]
        pf = p.astype(F32)
        dp = nt(gm, qkv[:, at_v])
        ds = (pf * (dp - jnp.sum(pf * dp, axis=1, keepdims=True)) * SCALE)
        q_h, k_h = qkv[:, at], qkv[:, at_k]
        qkv[:, at_v] = nn(pf.T.astype(BF16), gm).astype(BF16)
        qkv[:, at] = nn(ds.astype(BF16), k_h).astype(BF16)
        qkv[:, at_k] = nn(ds.T.astype(BF16), q_h).astype(BF16)
        if h in after:
            after[h]()
    r_env()
    for i in range(4):
        at = slice(256 * i, 256 * i + 256)
        gnorm[:, at] = nt(qkv[...], wqkv[at, :]) * gain_t_v[:, at]
    gy = gnorm[...]
    x = hid[...].astype(F32)
    inv_t = lax.rsqrt(jnp.mean(x * x, axis=1, keepdims=True) + 1e-6)
    pull = jnp.mean(x * gy, axis=1, keepdims=True) * (inv_t * inv_t * inv_t)
    igrad_o[...] = (gh[...].astype(F32) + gy * inv_t - x * pull).astype(BF16)
    u_end()
    r_end()


def hand_on(*refs):
    for i in range(4):
        refs[4 + i][...] = refs[i][...]


def per_device(
    hidden, done_step, alive, targets, gain_t, w_qkv_t, w_out_t, gain_a, w_qkv_a, w_out_a, w_value
):
    vmem = pl.BlockSpec(memory_space=pltpu.VMEM)
    away = pl.BlockSpec(memory_space=pl.ANY)
    mem = pltpu.VMEM
    dma = pltpu.SemaphoreType.DMA
    tile = (8, 128)
    scratch = [
        mem((STEPS, D), BF16), mem((D, 3 * D), BF16), mem((D, D), BF16), mem((STEPS, D), BF16),
        mem((STEPS, 3 * D), BF16), mem((HEADS, STEPS, STEPS), BF16), mem((STEPS, D), BF16),
        mem((4, 256, 256), BF16), mem((1024, 256), BF16), mem((1024, 256), BF16),
        mem((STEPS, D), BF16),
        mem((2, 2, 2, 2, 8, 64, 256), BF16), mem((8, *tile), F32), mem((8, *tile), F32),
        mem((2, 4, *tile), F32), mem((8, 2, *tile), F32), mem((128, D), BF16),
        mem((STEPS, D), BF16), mem((2, D, STEPS), BF16), mem((2, STEPS, D), BF16),
        mem((HEADS, 2, 128, 128), F32), mem((2, STEPS, D), BF16), mem((STEPS, D), BF16),
        mem((HEADS, STEPS), F32), mem((STEPS, D), F32), mem((256, 1024), BF16),
        mem((1024, 256), BF16), mem((1024, 256), BF16), mem((STEPS, D), BF16),
        mem((2, 2, 2, 8, 64, 256), BF16), mem((2, 2, 2, 4, 16, 256), BF16),
        mem((2, 4, 64, 256), BF16), mem((2, 2, 2, 8, 16, 256), BF16), mem((2, 8, 64, 256), BF16), mem((2, 2, 8, 16, 256), BF16), mem((8, 64, 256), BF16),
        mem((3, 8, 16, 256), BF16), mem((3, 8, 16, 256), BF16), mem((2, 8, 16, 256), BF16),
        mem((7, 2, 16, 256), BF16), mem((4, 2, 16, 256), F32),
        mem((8, 2, *tile), F32), mem((7, 2, *tile), F32), mem((2, *tile), F32),
        mem((7, *tile), F32), mem(tile, F32), mem((3, *tile), F32), mem(tile, F32),
        mem((7, *tile), F32), mem(tile, F32), mem((7, *tile), F32),
        dma((8,)), dma((31,)), dma((31,)), dma((1,)), dma((1,)), dma((1,)), dma((1,)),
        dma((59,)), dma((59,)), dma((28,)), dma((28,)),
    ]
    shapes = (
            jax.ShapeDtypeStruct((4, AGENTS), F32),
            jax.ShapeDtypeStruct((STEPS, D), BF16),
            jax.ShapeDtypeStruct((16, 3 * D), F32),
            jax.ShapeDtypeStruct((16, D), F32),
    )
    results = pl.pallas_call(
        kernel,
        out_shape=shapes,
        in_specs=[away, vmem, vmem, vmem, vmem, away, away, vmem, vmem, vmem, vmem],
        out_specs=(vmem, vmem, vmem, vmem),
        scratch_shapes=scratch,
        compiler_params=pltpu.CompilerParams(
            collective_id=0, has_side_effects=True, vmem_limit_bytes=60 * 2**20
        ),
    )(
        hidden[0, 0], done_step, alive[0].T, targets[0].T, gain_t[None], w_qkv_t, w_out_t, gain_a[None], w_qkv_a,
        w_out_a, w_value[None],
    )
    values, input_grad, qkv_grad, out_grad = pl.pallas_call(
        hand_on, out_shape=shapes, in_specs=[vmem] * 4, out_specs=(vmem,) * 4
    )(*results)
    return values.T[None], input_grad[None, None], qkv_grad, out_grad


def solution(mesh):
    in_specs = (
        P("env", "tm", None, None),
        P("env", "tm"),
        P("env", None, "tm"),
        P("env", None, "tm"),
        P(),
        P(),
        P(),
        P(),
        P("tm", None),
        P("tm", None),
        P(),
    )
    out_specs = (P("env", None, "tm"), P("env", "tm", None, None), P("tm", None), P("tm", None))
    return jax.shard_map(
        per_device, mesh=mesh, in_specs=in_specs, out_specs=out_specs, check_vma=False
    )
```

```python
import math

import jax
import jax.numpy as jnp
from jax import lax
from jax.experimental import pallas as pl
from jax.experimental.pallas import tpu as pltpu
from jax.sharding import PartitionSpec as P

F32, BF16 = jnp.float32, jnp.bfloat16
HEADS, D, STEPS, AGENTS = 8, 1024, 256, 64
HD = D // HEADS
SCALE = 1.0 / math.sqrt(HD)
NEG = -1e30
BAR, V2_AT, G2_AT = 4, 2, 7


def dot(a, b, ca, cb):
    return lax.dot_general(a, b, (((ca,), (cb,)), ((), ())), preferred_element_type=F32)


def nn(a, b):
    return dot(a, b, 1, 0)


def nt(a, b):
    return dot(a, b, 1, 1)


def tn(a, b):
    return dot(a, b, 0, 0)


def iota(shape, axis):
    return lax.broadcasted_iota(jnp.int32, shape, axis)


def split(x):
    high = x.astype(BF16)
    return high, (x - high.astype(F32)).astype(BF16)


def pick(condition):
    return jnp.where(condition, 1.0, 0.0).astype(BF16)


def step_to_block(flip):
    i, c = iota((256, 256), 1 if flip else 0), iota((256, 256), 0 if flip else 1)
    return pick(((i // 4) % 4 == c // 64) & (c % 64 == (i // 16) * 4 + i % 4))


def block_to_agent(flip):
    i, c = iota((256, 256), 1 if flip else 0), iota((256, 256), 0 if flip else 1)
    return pick((i % 16 == c // 16) & (i // 16 == c % 16))


def kernel(
    hidden_h, done_v, alive_v, target_v, gain_t_v, wqkv_h, wout_h, gain_a_v, wqkva_v, wouta_v, wval_v,
    values_o, igrad_o, qkvg_o, outg_o,
    hid, wqkv, wout, norm_t, qkv, prob_t, mixed, stage1, a1, r1, xr,
    w2, vb1, vb2, zb1, zb2, z128, na, nat, qk, prob_a, dqk, dqr, trow, gnorm, stage2, a2, r2, gh,
    tb, opp_y, opp_x, p1y, p1x, s1, s2, p2x, p2y, s3, pz, eb, us1, uz, um, uxy, uf, ue, up, uq, uw, ux,
    lsem, gs, gr, as1, ar1, as2, ar2, ss, sr, rs, rr,
):
    me, env = lax.axis_index("tm"), lax.axis_index("env")
    core, xl = env % 2, env // 2
    xh, z, y = me // 32, (me // 4) % 8, me % 4
    x_at = xh * 2 + xl
    core_id = {"env": env + 1 - 2 * core}

    def tm_at(xh_, z_, y_):
        return {"tm": xh_ * 32 + z_ * 4 + y_}

    def x_of(i):
        to = (x_at + i) % 4
        return to // 2, to % 2

    def x_peer(i):
        to_h, to_l = x_of(i)
        return {"env": to_l * 2 + core, "tm": to_h * 32 + z * 4 + y}

    def y_peer(i):
        return tm_at(xh, z, (y + i) % 4)

    def z_peer(i):
        return tm_at(xh, (z + i) % 8, y)

    def xy_of(i):
        to = (xh * 4 + y + i) % 8
        return to // 4, to % 4

    def xy_peer(i):
        to_h, to_y = xy_of(i)
        return tm_at(to_h, z, to_y)

    def send(src, dst, sems, k, where):
        copy = pltpu.make_async_remote_copy(
            src_ref=src, dst_ref=dst, send_sem=sems[0].at[k], recv_sem=sems[1].at[k],
            device_id=where, device_id_type=pl.DeviceIdType.MESH,
        )
        copy.start()
        return copy

    def spread(body):
        def step(i, carry):
            body(lax.rem(me + i, 64))
            return carry
        lax.fori_loop(1, 64, step, 0)

    barrier = pltpu.get_barrier_semaphore()

    def greet(where):
        pl.semaphore_signal(
            barrier, inc=1, device_id=where, device_id_type=pl.DeviceIdType.MESH
        )

    for i in range(1, 8):
        greet(z_peer(i))
    for i in range(1, 8):
        greet(xy_peer(i))
    greet({"env": (env + 2) % 4, "tm": (1 - xh) * 32 + z * 4 + y})
    for i in (1, 2, 3):
        greet({"env": (env + i) % 4})

    loads = [pltpu.make_async_copy(hidden_h, hid, lsem.at[0])]
    for j in range(6):
        at = (slice(None), slice(512 * j, 512 * j + 512))
        loads.append(pltpu.make_async_copy(wqkv_h.at[at], wqkv.at[at], lsem.at[1 + j]))
    loads.append(pltpu.make_async_copy(wout_h, wout, lsem.at[7]))
    for load in loads:
        load.start()

    w_value = wval_v[...]
    lane_off = (me % 8) * 16
    spot = iota((16, 128), 1) == iota((16, 128), 0) + lane_off
    own_line = iota((8, 128), 0) == me // 8

    def to_lanes(column):
        return jnp.sum(jnp.where(spot, column, 0.0), axis=0, keepdims=True)

    def rows_of(y_):
        return pl.ds(pl.multiple_of(y_ * 16, 16), 16)

    own_rows = rows_of(y)
    for half in range(2):
        at = pl.multiple_of(core * D + half * 512 + xl * 256, 256)
        w2[core, half, xl, xh, z, own_rows, :] = wqkva_v[:, pl.ds(at, 256)]
    v_part = jnp.sum(wouta_v[...].astype(F32) * w_value, axis=1, keepdims=True)
    vb1[0] = jnp.where(own_line, to_lanes(v_part), 0.0)

    G, S, R = (gs, gr), (ss, sr), (rs, rr)
    both, every = pl.ds(0, 2), pl.ds(0, 8)
    live = {}

    def begin(name, i, *what):
        live[(name, i)] = send(*what)

    def finish(name, n):
        for i in range(1, n + 1):
            live[(name, i)].wait()

    def g_z():
        ref = w2.at[core, both, xl, xh, z, own_rows]
        for i in range(1, 8):
            begin("gz", i, ref, ref, G, i - 1, z_peer(i))

    def g_2():
        finish("gz", 7)
        for i in (1, 2, 3):
            for half, peer, k in ((0, x_peer(i), 6), (1, y_peer(i), 9)):
                ref = w2.at[core, half, xl, xh, every, own_rows]
                begin(f"g2{half}", i, ref, ref, G, k + i, peer)

    def to_core(k, ref):
        begin("gc", k + 1, ref, ref, G, 21 + k, core_id)

    first, second = pl.ds(0, 4), pl.ds(4, 4)

    def y_piece(i, zs_=every):
        return w2.at[core, 0, both, both, zs_, rows_of((y + i) % 4)]

    def x_piece(i, zs_=every):
        to_h, to_l = x_of(i)
        return w2.at[core, 1, to_l, to_h, zs_]

    def g_3():
        for half, part, peer in ((0, y_piece, y_peer), (1, x_piece, x_peer)):
            finish(f"g2{half}", 3)
            for i in (1, 3):
                begin(f"g3{half}", i, part(0), part(0), G, 13 + 4 * half + i // 2, peer(i))
            to_core(4 * half, part(0))

    def g_mid():
        for half, part, peer in ((0, y_piece, y_peer), (1, x_piece, x_peer)):
            for i, zs_ in ((1, first), (3, second)):
                live[(f"g3{half}", i)].wait()
                ref = part(4 - i, zs_)
                begin(f"g4{half}", i, ref, ref, G, 15 + 4 * half + i // 2, peer(i))
        for half, part in ((0, y_piece), (1, x_piece)):
            for i in (1, 3):
                to_core(4 * half + 1 + i // 2, part(4 - i))

    def g_end():
        for half, part in ((0, y_piece), (1, x_piece)):
            for i in (1, 3):
                live[(f"g4{half}", i)].wait()
            to_core(4 * half + 3, part(2))

    def v_1():
        for i in range(1, 8):
            begin("v1", i, vb1.at[0], vb1.at[i], S, i - 1, xy_peer(i))

    def v_2():
        finish("v1", 7)
        vb2[0] = jnp.sum(vb1[...], axis=0)
        for i in range(1, 8):
            begin("v2", i, vb2.at[0], vb2.at[i], S, 6 + i, z_peer(i))

    def z_1():
        finish("v2", 7)
        v8 = jnp.sum(vb2[...], axis=0)
        rows = []
        for h in range(HEADS):
            w_v = wqkva_v[:, 2 * D + h * HD : 2 * D + (h + 1) * HD].astype(F32)
            col = jnp.sum(w_v * v8[h : h + 1, :], axis=1, keepdims=True)
            rows.append(to_lanes(col))
        zb1[xh, y] = jnp.concatenate(rows, axis=0)
        for i in range(1, 8):
            begin("z1", i, zb1.at[xh, y], zb1.at[xh, y], S, 13 + i, xy_peer(i))

    def z_2():
        finish("z1", 7)
        zb2[z] = jnp.sum(zb1[...], axis=1)
        for i in range(1, 8):
            begin("z2", i, zb2.at[z], zb2.at[z], S, 20 + i, z_peer(i))

    def z_end():
        finish("z2", 7)
        tiles = []
        for i in range(2):
            for j in range(4):
                tiles.append(zb2[2 * j, i] + zb2[2 * j + 1, i])
        z_hi, z_lo = split(jnp.concatenate(tiles, axis=1))
        z128[...] = jnp.zeros((128, D), BF16)
        z128[0:16, :] = jnp.concatenate([z_hi, z_hi], axis=0)
        z128[16:32, :] = jnp.concatenate([z_lo, jnp.zeros_like(z_lo)], axis=0)

    loads[0].wait()
    x = hid[...].astype(F32)
    inv_t = lax.rsqrt(jnp.mean(x * x, axis=1, keepdims=True) + 1e-6)
    norm_t[...] = (x * inv_t * gain_t_v[...]).astype(BF16)
    for j in range(6):
        loads[1 + j].wait()
        at = slice(512 * j, 512 * j + 512)
        qkv[:, at] = nn(norm_t[...], wqkv[:, at]).astype(BF16)
        if j == BAR:
            pl.semaphore_wait(barrier, 18)
            g_z()
            v_1()
    done = done_v[...]
    ri, ci = iota((STEPS, STEPS), 0), iota((STEPS, STEPS), 1)
    allowed_t = (ri >= ci) & ((ri > done) == (ci > done))
    for h in range(HEADS):
        at = slice(h * HD, (h + 1) * HD)
        s = nt(qkv[:, at], qkv[:, D + h * HD : D + (h + 1) * HD]) * SCALE
        s = jnp.where(allowed_t, s, NEG)
        e = jnp.exp(s - jnp.max(s, axis=1, keepdims=True))
        p = (e * (1.0 / jnp.sum(e, axis=1, keepdims=True))).astype(BF16)
        prob_t[h] = p
        mixed[:, at] = nn(p, qkv[:, 2 * D + h * HD : 2 * D + (h + 1) * HD]).astype(BF16)
        if h == V2_AT:
            v_2()
        if h == G2_AT:
            g_2()
    loads[7].wait()
    turn = step_to_block(False)
    for q in range(4):
        at = slice(256 * q, 256 * q + 256)
        h1 = (hid[:, at].astype(F32) + nn(mixed[...], wout[:, at])).astype(BF16)
        for j in range(4):
            stage1[j, q * 64 : q * 64 + 64, :] = h1[j * 64 : j * 64 + 64, :]
    for j in range(4):
        a1[j * 256 : j * 256 + 256, :] = nn(turn, stage1[j]).astype(BF16)

    def block(peer):
        return pl.ds(pl.multiple_of(peer * 16, 16), 16)

    def put_1(peer):
        send(a1.at[block(peer)], r1.at[block(me)], (as1, ar1), 0, {"tm": peer})

    spread(put_1)
    r1[block(me), :] = a1[block(me), :]

    def wait_all(src, dst, sems):
        pltpu.make_async_remote_copy(
            src_ref=src.at[pl.ds(0, 1008)], dst_ref=dst.at[pl.ds(0, 1008)], send_sem=sems[0].at[0],
            recv_sem=sems[1].at[0], device_id=core_id, device_id_type=pl.DeviceIdType.MESH,
        ).wait()

    g_3()
    z_1()
    z_2()
    g_mid()
    z_end()
    wait_all(a1, r1, (as1, ar1))

    unturn = block_to_agent(False)
    for j in range(4):
        got = nn(unturn, r1[j * 256 : j * 256 + 256, :]).astype(BF16)
        for q in range(4):
            for s in range(4):
                i = (q * 4 + s) * 16
                xr[s * 64 + j * 16 : s * 64 + j * 16 + 16, q * 256 : q * 256 + 256] = got[
                    i : i + 16, :
                ]
    xa = xr[...].astype(F32)
    inv_a = lax.rsqrt(jnp.mean(xa * xa, axis=1, keepdims=True) + 1e-6)
    h1_value = jnp.sum(xa * w_value, axis=1, keepdims=True)
    normed = xa * inv_a * gain_a_v[...]
    na[...] = normed.astype(BF16)
    for j in range(4):
        nat[0, j * 256 : j * 256 + 256, :] = normed[:, j * 256 : j * 256 + 256].T.astype(BF16)
    begin("nat", 1, nat.at[0], nat.at[1], G, 29, core_id)
    s_rows = nt(z128[0:32, :], na[...])
    s_rows = s_rows[0:8] + s_rows[16:24]
    diag = ri == ci
    alive_f, target_f = alive_v[...].astype(F32), target_v[...]

    def one_row(table):
        return jnp.concatenate([table[s : s + 1, :] for s in range(4)], axis=1)

    def to_column(row):
        return jnp.sum(jnp.where(diag, row, 0.0), axis=1, keepdims=True)

    alive_row = one_row(alive_f)
    alive_col, target_col = to_column(alive_row), to_column(one_row(target_f))
    g_end()

    def project(which):
        for half in range(2):
            for l in range(2):
                at = half * 512 + l * 256
                w = w2[which, half, l].reshape(D, 256)
                qk[which, :, at : at + 256] = nn(na[...], w).astype(BF16)

    project(core)
    finish("gc", 8)
    project(1 - core)
    square = iota((128, 128), 0), iota((128, 128), 1)
    same_step = (square[0] // 64) == (square[1] // 64)
    sums = []
    for p in range(2):
        rows = slice(128 * p, 128 * p + 128)
        seen = same_step & ((alive_row[:, rows] == 1.0) | (square[0] == square[1]))
        total = jnp.zeros((128, 1), F32)
        for h in range(HEADS):
            at = slice(h * HD, (h + 1) * HD)
            s = nt(qk[0, rows, at], qk[1, rows, at]) * SCALE
            s = jnp.where(seen, s, NEG)
            e = jnp.exp(s - jnp.max(s, axis=1, keepdims=True))
            e = e * (1.0 / jnp.sum(e, axis=1, keepdims=True))
            prob_a[h, p] = e
            total = total + jnp.sum(e * s_rows[h : h + 1, rows], axis=1, keepdims=True)
        sums.append(total)
    predicted = h1_value + jnp.concatenate(sums, axis=0)
    err = 32.0 * alive_col * (predicted - target_col)
    line = jnp.sum(jnp.where(diag, predicted, 0.0), axis=0, keepdims=True)
    for s in range(4):
        values_o[s : s + 1, :] = line[:, s * 64 : s * 64 + 64]
    for p in range(2):
        rows = pl.ds(128 * p, 128)
        for h in range(HEADS):
            at = slice(h * HD, (h + 1) * HD)
            e = prob_a[h, p]
            s_row = s_rows[h : h + 1, 128 * p : 128 * p + 128]
            pv = jnp.sum(e * s_row, axis=1, keepdims=True)
            weighted = e * err[128 * p : 128 * p + 128, :]
            trow[h : h + 1, rows] = jnp.sum(weighted, axis=0, keepdims=True)
            ds = weighted * (s_row - pv) * SCALE
            dqk[0, rows, at] = nn(ds.astype(BF16), qk[1, rows, at]).astype(BF16)
            dqk[1, rows, at] = nn(ds.T.astype(BF16), qk[0, rows, at]).astype(BF16)
        begin("dqk", p + 1, dqk.at[1 - core, rows], dqr.at[rows], G, 30 + p, core_id)

    t_hi = trow[...].astype(BF16).astype(F32)
    t_lo = trow[...] - t_hi
    u_all = nn(jnp.concatenate([t_hi, t_lo], axis=0).astype(BF16), na[...])
    u_all = u_all[0:8] + u_all[8:16]
    for i in range(8):
        for j in range(2):
            at = (j * 4 + i // 2) * 128
            us1[i, j] = u_all[:, at : at + 128]
    for i in range(1, 8):
        begin("uz", i, us1.at[(z + i) % 8], uz.at[i - 1], S, 27 + i, z_peer(i))

    t_all = jnp.concatenate([t_hi, t_lo, t_hi, jnp.zeros((104, STEPS), F32)], axis=0)
    t_col = t_all.T.astype(BF16)
    for i in range(4):
        at = slice(256 * i, 256 * i + 256)
        part = nn(t_col, z128[:, at])
        for c in range(2):
            for half in range(2):
                for l in range(2):
                    w = w2[c, half, l, i // 2, 4 * (i % 2) : 4 * (i % 2) + 4].reshape(256, 256)
                    lanes = half * 512 + l * 256
                    part = part + nt(dqk[c, :, lanes : lanes + 256], w)
        gnorm[:, at] = part * gain_a_v[:, at]

    peers, opp = (y_peer, x_peer), (opp_y, opp_x)

    def term(half, i, zs_):
        if half == 0:
            return tb.at[0, both, both, zs_, rows_of((y + i) % 4)]
        to_h, to_l = x_of(i)
        return tb.at[1, to_l, to_h, zs_]

    def got_1(half, n, zs_):
        return p1y.at[n, both, both, zs_] if half == 0 else p1x.at[n, zs_]

    live[("nat", 1)].wait()
    finish("dqk", 2)
    for half in range(2):
        for l in range(2):
            at = half * 512 + l * 256
            part = nn(nat[0], dqk[core, :, at : at + 256]) + nn(nat[1], dqr[:, at : at + 256])
            tb[half, l] = part.astype(BF16).reshape(2, 8, 64, 256)
        for n, (i, across, plain) in enumerate(((1, first, second), (3, second, first))):
            begin(
                f"q{half}", i, term(half, 2, across), opp[half].at[n], R, 6 * half + n, peers[half](i)
            )
            begin(
                f"p{half}", i, term(half, i, plain), got_1(half, n, plain),
                R, 6 * half + 2 + n, peers[half](i),
            )

    gy = gnorm[...]
    xa = xr[...].astype(F32)
    pull = jnp.mean(xa * gy, axis=1, keepdims=True) * (inv_a * inv_a * inv_a)
    grad = (err * w_value + gy * inv_a - xa * pull).astype(BF16)
    turn = block_to_agent(True)
    for j in range(4):
        for q in range(4):
            for s in range(4):
                i = (q * 4 + s) * 16
                stage2[i : i + 16, j * 256 : j * 256 + 256] = grad[
                    s * 64 + j * 16 : s * 64 + j * 16 + 16, q * 256 : q * 256 + 256
                ]
    for j in range(4):
        a2[j * 256 : j * 256 + 256, :] = nn(turn, stage2[:, j * 256 : j * 256 + 256]).astype(BF16)

    def put_2(peer):
        send(a2.at[block(peer)], r2.at[block(me)], (as2, ar2), 0, {"tm": peer})

    spread(put_2)
    r2[block(me), :] = a2[block(me), :]

    def u_xy():
        finish("uz", 7)
        um[...] = us1[z] + jnp.sum(uz[...], axis=0)
        for i in range(1, 8):
            begin("uxy", i, um.at[xy_of(i)[0]], uxy.at[i - 1], S, 34 + i, xy_peer(i))

    def u_env():
        finish("uxy", 7)
        uf[...] = um[xh] + jnp.sum(uxy[...], axis=0)
        for i in (1, 2, 3):
            begin("ue", i, uf, ue.at[i - 1], S, 41 + i, {"env": (env + i) % 4})

    def u_mix():
        finish("ue", 3)
        u = uf[...] + jnp.sum(ue[...], axis=0)
        v8 = jnp.sum(vb2[...], axis=0)
        lines = []
        for h in range(HEADS):
            at = slice(2 * D + h * HD, 2 * D + (h + 1) * HD)
            col = jnp.sum(jnp.where(spot, u[h : h + 1, :], 0.0), axis=1, keepdims=True)
            qkvg_o[:, at] = col * v8[h : h + 1, :]
            lines.append(jnp.sum(col * wqkva_v[:, at].astype(F32), axis=0, keepdims=True))
        up[...] = jnp.concatenate(lines, axis=0)
        for i in range(1, 8):
            begin("uq", i, up, uq.at[i - 1], S, 44 + i, z_peer(i))

    def u_last():
        finish("uq", 7)
        uw[...] = up[...] + jnp.sum(uq[...], axis=0)
        for i in range(1, 8):
            begin("ux", i, uw, ux.at[i - 1], S, 51 + i, xy_peer(i))

    def u_end():
        finish("ux", 7)
        total = uw[...] + jnp.sum(ux[...], axis=0)
        row = jnp.sum(jnp.where(own_line, total, 0.0), axis=0, keepdims=True)
        outg_o[...] = jnp.sum(jnp.where(spot, row, 0.0), axis=1, keepdims=True) * w_value

    def r_1():
        for half in range(2):
            for n, (i, across) in enumerate(((1, first), (3, second))):
                live[(f"q{half}", i)].wait()
                z0 = 4 * n
                if half == 0:
                    rows = rows_of((y + i) % 4)
                    for l in range(2):
                        for k in range(2):
                            both_terms = tb[0, l, k, z0 : z0 + 4, rows, :] + opp_y[n, l, k]
                            tb[0, l, k, z0 : z0 + 4, rows, :] = both_terms
                else:
                    to_h, to_l = x_of(i)
                    for k in range(4):
                        tb[1, to_l, to_h, z0 + k] = tb[1, to_l, to_h, z0 + k] + opp_x[n, k]
                begin(
                    f"r{half}", i, term(half, i, across), got_1(half, n, across),
                    R, 6 * half + 4 + n, peers[half](i),
                )

    def r_2():
        for name in ("p0", "r0"):
            for i in (1, 3):
                live[(name, i)].wait()
        for l in range(2):
            for i in range(2):
                total = tb[0, l, i, :, own_rows, :].astype(F32)
                for k in range(2):
                    total = total + p1y[k, l, i].astype(F32)
                s1[l, i] = total.astype(BF16)
        for i in (1, 2, 3):
            to_h, to_l = x_of(i)
            begin("p2x", i, s1.at[to_l, to_h], p2x.at[i - 1], R, 11 + i, x_peer(i))
        for name in ("p1", "r1"):
            for i in (1, 3):
                live[(name, i)].wait()
        for i in range(8):
            total = tb[1, xl, xh, i].astype(F32)
            for k in range(2):
                total = total + p1x[k, i].astype(F32)
            s2[i] = total.astype(BF16)
        for i in (1, 2, 3):
            begin(
                "p2y", i, s2.at[every, rows_of((y + i) % 4)], p2y.at[i - 1], R, 14 + i, y_peer(i)
            )

    def r_z():
        finish("p2x", 3)
        total = s1[xl, xh].astype(F32)
        for k in range(3):
            total = total + p2x[k].astype(F32)
        s3[0] = total.astype(BF16)
        finish("p2y", 3)
        total = s2[:, own_rows, :].astype(F32)
        for k in range(3):
            total = total + p2y[k].astype(F32)
        s3[1] = total.astype(BF16)
        for i in range(1, 8):
            begin("pz", i, s3.at[both, (z + i) % 8], pz.at[i - 1], R, 17 + i, z_peer(i))

    def r_env():
        finish("pz", 7)
        total = s3[:, z].astype(F32)
        for k in range(7):
            total = total + pz[k].astype(F32)
        eb[env] = total
        for i in (1, 2, 3):
            begin("eb", i, eb.at[env], eb.at[env], R, 24 + i, {"env": (env + i) % 4})

    def r_end():
        finish("eb", 3)
        for e in range(4):
            for half in range(2):
                at = (e % 2) * D + half * 512 + (e // 2) * 256
                qkvg_o[:, at : at + 256] = eb[e, half]

    r_1()
    u_xy()
    r_2()
    u_env()

    wait_all(a2, r2, (as2, ar2))
    unturn = step_to_block(True)
    for j in range(4):
        got = nn(unturn, r2[j * 256 : j * 256 + 256, :]).astype(BF16)
        for q in range(4):
            gh[j * 64 : j * 64 + 64, q * 256 : q * 256 + 256] = got[q * 64 : q * 64 + 64, :]
    after = {1: r_z, 2: u_mix, 5: u_last}
    for h in range(HEADS):
        at = slice(h * HD, (h + 1) * HD)
        at_k, at_v = slice(D + h * HD, D + (h + 1) * HD), slice(2 * D + h * HD, 2 * D + (h + 1) * HD)
        gm = nt(gh[...], wout[at, :]).astype(BF16)
        p = prob_t[h]
        pf = p.astype(F32)
        dp = nt(gm, qkv[:, at_v])
        ds = (pf * (dp - jnp.sum(pf * dp, axis=1, keepdims=True)) * SCALE)
        q_h, k_h = qkv[:, at], qkv[:, at_k]
        qkv[:, at_v] = nn(pf.T.astype(BF16), gm).astype(BF16)
        qkv[:, at] = nn(ds.astype(BF16), k_h).astype(BF16)
        qkv[:, at_k] = nn(ds.T.astype(BF16), q_h).astype(BF16)
        if h in after:
            after[h]()
    r_env()
    for i in range(4):
        at = slice(256 * i, 256 * i + 256)
        gnorm[:, at] = nt(qkv[...], wqkv[at, :]) * gain_t_v[:, at]
    gy = gnorm[...]
    x = hid[...].astype(F32)
    inv_t = lax.rsqrt(jnp.mean(x * x, axis=1, keepdims=True) + 1e-6)
    pull = jnp.mean(x * gy, axis=1, keepdims=True) * (inv_t * inv_t * inv_t)
    igrad_o[...] = (gh[...].astype(F32) + gy * inv_t - x * pull).astype(BF16)
    u_end()
    r_end()


def hand_on(*refs):
    for i in range(4):
        refs[4 + i][...] = refs[i][...]


def per_device(
    hidden, done_step, alive, targets, gain_t, w_qkv_t, w_out_t, gain_a, w_qkv_a, w_out_a, w_value
):
    vmem = pl.BlockSpec(memory_space=pltpu.VMEM)
    away = pl.BlockSpec(memory_space=pl.ANY)
    mem = pltpu.VMEM
    dma = pltpu.SemaphoreType.DMA
    tile = (8, 128)
    scratch = [
        mem((STEPS, D), BF16), mem((D, 3 * D), BF16), mem((D, D), BF16), mem((STEPS, D), BF16),
        mem((STEPS, 3 * D), BF16), mem((HEADS, STEPS, STEPS), BF16), mem((STEPS, D), BF16),
        mem((4, 256, 256), BF16), mem((1024, 256), BF16), mem((1024, 256), BF16),
        mem((STEPS, D), BF16),
        mem((2, 2, 2, 2, 8, 64, 256), BF16), mem((8, *tile), F32), mem((8, *tile), F32),
        mem((2, 4, *tile), F32), mem((8, 2, *tile), F32), mem((128, D), BF16),
        mem((STEPS, D), BF16), mem((2, D, STEPS), BF16), mem((2, STEPS, D), BF16),
        mem((HEADS, 2, 128, 128), F32), mem((2, STEPS, D), BF16), mem((STEPS, D), BF16),
        mem((HEADS, STEPS), F32), mem((STEPS, D), F32), mem((256, 1024), BF16),
        mem((1024, 256), BF16), mem((1024, 256), BF16), mem((STEPS, D), BF16),
        mem((2, 2, 2, 8, 64, 256), BF16), mem((2, 2, 2, 4, 16, 256), BF16),
        mem((2, 4, 64, 256), BF16), mem((2, 2, 2, 8, 16, 256), BF16), mem((2, 8, 64, 256), BF16), mem((2, 2, 8, 16, 256), BF16), mem((8, 64, 256), BF16),
        mem((3, 8, 16, 256), BF16), mem((3, 8, 16, 256), BF16), mem((2, 8, 16, 256), BF16),
        mem((7, 2, 16, 256), BF16), mem((4, 2, 16, 256), F32),
        mem((8, 2, *tile), F32), mem((7, 2, *tile), F32), mem((2, *tile), F32),
        mem((7, *tile), F32), mem(tile, F32), mem((3, *tile), F32), mem(tile, F32),
        mem((7, *tile), F32), mem(tile, F32), mem((7, *tile), F32),
        dma((8,)), dma((32,)), dma((32,)), dma((1,)), dma((1,)), dma((1,)), dma((1,)),
        dma((59,)), dma((59,)), dma((28,)), dma((28,)),
    ]
    shapes = (
            jax.ShapeDtypeStruct((4, AGENTS), F32),
            jax.ShapeDtypeStruct((STEPS, D), BF16),
            jax.ShapeDtypeStruct((16, 3 * D), F32),
            jax.ShapeDtypeStruct((16, D), F32),
    )
    results = pl.pallas_call(
        kernel,
        out_shape=shapes,
        in_specs=[away, vmem, vmem, vmem, vmem, away, away, vmem, vmem, vmem, vmem],
        out_specs=(vmem, vmem, vmem, vmem),
        scratch_shapes=scratch,
        compiler_params=pltpu.CompilerParams(
            collective_id=0, has_side_effects=True, vmem_limit_bytes=60 * 2**20
        ),
    )(
        hidden[0, 0], done_step, alive[0].T, targets[0].T, gain_t[None], w_qkv_t, w_out_t, gain_a[None], w_qkv_a,
        w_out_a, w_value[None],
    )
    values, input_grad, qkv_grad, out_grad = pl.pallas_call(
        hand_on, out_shape=shapes, in_specs=[vmem] * 4, out_specs=(vmem,) * 4
    )(*results)
    return values.T[None], input_grad[None, None], qkv_grad, out_grad


def solution(mesh):
    in_specs = (
        P("env", "tm", None, None),
        P("env", "tm"),
        P("env", None, "tm"),
        P("env", None, "tm"),
        P(),
        P(),
        P(),
        P(),
        P("tm", None),
        P("tm", None),
        P(),
    )
    out_specs = (P("env", None, "tm"), P("env", "tm", None, None), P("tm", None), P("tm", None))
    return jax.shard_map(
        per_device, mesh=mesh, in_specs=in_specs, out_specs=out_specs, check_vma=False
    )
```

```python
import math

import jax
import jax.numpy as jnp
from jax import lax
from jax.experimental import pallas as pl
from jax.experimental.pallas import tpu as pltpu
from jax.sharding import PartitionSpec as P

F32, BF16 = jnp.float32, jnp.bfloat16
HEADS, D, STEPS, AGENTS = 8, 1024, 256, 64
HD = D // HEADS
SCALE = 1.0 / math.sqrt(HD)
NEG = -1e30
BAR, V2_AT, G2_AT = 4, 2, 7


def dot(a, b, ca, cb):
    return lax.dot_general(a, b, (((ca,), (cb,)), ((), ())), preferred_element_type=F32)


def nn(a, b):
    return dot(a, b, 1, 0)


def nt(a, b):
    return dot(a, b, 1, 1)


def tn(a, b):
    return dot(a, b, 0, 0)


def iota(shape, axis):
    return lax.broadcasted_iota(jnp.int32, shape, axis)


def split(x):
    high = x.astype(BF16)
    return high, (x - high.astype(F32)).astype(BF16)


def pick(condition):
    return jnp.where(condition, 1.0, 0.0).astype(BF16)


def step_to_block(flip):
    i, c = iota((256, 256), 1 if flip else 0), iota((256, 256), 0 if flip else 1)
    return pick(((i // 4) % 4 == c // 64) & (c % 64 == (i // 16) * 4 + i % 4))


def block_to_agent(flip):
    i, c = iota((256, 256), 1 if flip else 0), iota((256, 256), 0 if flip else 1)
    return pick((i % 16 == c // 16) & (i // 16 == c % 16))


def kernel(
    hidden_h, done_v, alive_v, target_v, gain_t_v, wqkv_h, wout_h, gain_a_v, wqkva_v, wouta_v, wval_v,
    values_o, igrad_o, qkvg_o, outg_o,
    hid, wqkv, wout, norm_t, qkv, prob_t, mixed, stage1, a1, r1, xr,
    w2, vb1, vb2, zb1, zb2, z128, na, nat, qk, prob_a, dqk, dqr, trow, gnorm, stage2, a2, r2, gh,
    tb, opp_y, opp_x, p1y, p1x, s1, s2, p2x, p2y, s3, pz, eb, us1, uz, um, uxy, uf, ue, up, uq, uw, ux,
    lsem, gs, gr, as1, ar1, as2, ar2, ss, sr, rs, rr,
):
    me, env = lax.axis_index("tm"), lax.axis_index("env")
    core, xl = env % 2, env // 2
    xh, z, y = me // 32, (me // 4) % 8, me % 4
    x_at = xh * 2 + xl
    core_id = {"env": env + 1 - 2 * core}

    def tm_at(xh_, z_, y_):
        return {"tm": xh_ * 32 + z_ * 4 + y_}

    def x_of(i):
        to = (x_at + i) % 4
        return to // 2, to % 2

    def x_peer(i):
        to_h, to_l = x_of(i)
        return {"env": to_l * 2 + core, "tm": to_h * 32 + z * 4 + y}

    def y_peer(i):
        return tm_at(xh, z, (y + i) % 4)

    def z_peer(i):
        return tm_at(xh, (z + i) % 8, y)

    def xy_of(i):
        to = (xh * 4 + y + i) % 8
        return to // 4, to % 4

    def xy_peer(i):
        to_h, to_y = xy_of(i)
        return tm_at(to_h, z, to_y)

    def send(src, dst, sems, k, where):
        copy = pltpu.make_async_remote_copy(
            src_ref=src, dst_ref=dst, send_sem=sems[0].at[k], recv_sem=sems[1].at[k],
            device_id=where, device_id_type=pl.DeviceIdType.MESH,
        )
        copy.start()
        return copy

    def spread(body):
        def step(i, carry):
            body(lax.rem(me + i, 64))
            return carry
        lax.fori_loop(1, 64, step, 0)

    barrier = pltpu.get_barrier_semaphore()

    def greet(where):
        pl.semaphore_signal(
            barrier, inc=1, device_id=where, device_id_type=pl.DeviceIdType.MESH
        )

    for i in range(1, 8):
        greet(z_peer(i))
    for i in range(1, 8):
        greet(xy_peer(i))
    greet({"env": (env + 2) % 4, "tm": (1 - xh) * 32 + z * 4 + y})
    for i in (1, 2, 3):
        greet({"env": (env + i) % 4})

    loads = [pltpu.make_async_copy(hidden_h, hid, lsem.at[0])]
    for j in range(6):
        at = (slice(None), slice(512 * j, 512 * j + 512))
        loads.append(pltpu.make_async_copy(wqkv_h.at[at], wqkv.at[at], lsem.at[1 + j]))
    loads.append(pltpu.make_async_copy(wout_h, wout, lsem.at[7]))
    for load in loads:
        load.start()

    w_value = wval_v[...]
    lane_off = (me % 8) * 16
    spot = iota((16, 128), 1) == iota((16, 128), 0) + lane_off
    own_line = iota((8, 128), 0) == me // 8

    def to_lanes(column):
        return jnp.sum(jnp.where(spot, column, 0.0), axis=0, keepdims=True)

    def rows_of(y_):
        return pl.ds(pl.multiple_of(y_ * 16, 16), 16)

    own_rows = rows_of(y)
    for half in range(2):
        at = pl.multiple_of(core * D + half * 512 + xl * 256, 256)
        w2[core, half, xl, xh, z, own_rows, :] = wqkva_v[:, pl.ds(at, 256)]
    v_part = jnp.sum(wouta_v[...].astype(F32) * w_value, axis=1, keepdims=True)
    vb1[0] = jnp.where(own_line, to_lanes(v_part), 0.0)

    G, S, R = (gs, gr), (ss, sr), (rs, rr)
    both, every = pl.ds(0, 2), pl.ds(0, 8)
    live = {}

    def begin(name, i, *what):
        live[(name, i)] = send(*what)

    def finish(name, n):
        for i in range(1, n + 1):
            live[(name, i)].wait()

    def g_z():
        ref = w2.at[core, both, xl, xh, z, own_rows]
        for i in range(1, 8):
            begin("gz", i, ref, ref, G, i - 1, z_peer(i))

    def g_2():
        finish("gz", 7)
        for i in (1, 2, 3):
            for half, peer, k in ((0, x_peer(i), 6), (1, y_peer(i), 9)):
                ref = w2.at[core, half, xl, xh, every, own_rows]
                begin(f"g2{half}", i, ref, ref, G, k + i, peer)

    def to_core(k, ref):
        begin("gc", k + 1, ref, ref, G, 21 + k, core_id)

    first, second = pl.ds(0, 4), pl.ds(4, 4)

    def y_piece(i, zs_=every):
        return w2.at[core, 0, both, both, zs_, rows_of((y + i) % 4)]

    def x_piece(i, zs_=every):
        to_h, to_l = x_of(i)
        return w2.at[core, 1, to_l, to_h, zs_]

    def g_3():
        for half, part, peer in ((0, y_piece, y_peer), (1, x_piece, x_peer)):
            finish(f"g2{half}", 3)
            for i in (1, 3):
                begin(f"g3{half}", i, part(0), part(0), G, 13 + 4 * half + i // 2, peer(i))
            to_core(4 * half, part(0))

    def g_mid():
        for half, part, peer in ((0, y_piece, y_peer), (1, x_piece, x_peer)):
            for i, zs_ in ((1, first), (3, second)):
                live[(f"g3{half}", i)].wait()
                ref = part(4 - i, zs_)
                begin(f"g4{half}", i, ref, ref, G, 15 + 4 * half + i // 2, peer(i))
        for half, part in ((0, y_piece), (1, x_piece)):
            for i in (1, 3):
                to_core(4 * half + 1 + i // 2, part(4 - i))

    def g_end():
        for half, part in ((0, y_piece), (1, x_piece)):
            for i in (1, 3):
                live[(f"g4{half}", i)].wait()
            to_core(4 * half + 3, part(2))

    def v_1():
        for i in range(1, 8):
            begin("v1", i, vb1.at[0], vb1.at[i], S, i - 1, xy_peer(i))

    def v_2():
        finish("v1", 7)
        vb2[0] = jnp.sum(vb1[...], axis=0)
        for i in range(1, 8):
            begin("v2", i, vb2.at[0], vb2.at[i], S, 6 + i, z_peer(i))

    def z_1():
        finish("v2", 7)
        v8 = jnp.sum(vb2[...], axis=0)
        rows = []
        for h in range(HEADS):
            w_v = wqkva_v[:, 2 * D + h * HD : 2 * D + (h + 1) * HD].astype(F32)
            col = jnp.sum(w_v * v8[h : h + 1, :], axis=1, keepdims=True)
            rows.append(to_lanes(col))
        zb1[xh, y] = jnp.concatenate(rows, axis=0)
        for i in range(1, 8):
            begin("z1", i, zb1.at[xh, y], zb1.at[xh, y], S, 13 + i, xy_peer(i))

    def z_2():
        finish("z1", 7)
        zb2[z] = jnp.sum(zb1[...], axis=1)
        for i in range(1, 8):
            begin("z2", i, zb2.at[z], zb2.at[z], S, 20 + i, z_peer(i))

    def z_end():
        finish("z2", 7)
        tiles = []
        for i in range(2):
            for j in range(4):
                tiles.append(zb2[2 * j, i] + zb2[2 * j + 1, i])
        z_hi, z_lo = split(jnp.concatenate(tiles, axis=1))
        z128[...] = jnp.zeros((128, D), BF16)
        z128[0:16, :] = jnp.concatenate([z_hi, z_hi], axis=0)
        z128[16:32, :] = jnp.concatenate([z_lo, jnp.zeros_like(z_lo)], axis=0)

    loads[0].wait()
    x = hid[...].astype(F32)
    inv_t = lax.rsqrt(jnp.mean(x * x, axis=1, keepdims=True) + 1e-6)
    norm_t[...] = (x * inv_t * gain_t_v[...]).astype(BF16)
    for j in range(6):
        loads[1 + j].wait()
        at = slice(512 * j, 512 * j + 512)
        qkv[:, at] = nn(norm_t[...], wqkv[:, at]).astype(BF16)
        if j == BAR:
            pl.semaphore_wait(barrier, 18)
            g_z()
            v_1()
    done = done_v[...]
    ri, ci = iota((STEPS, STEPS), 0), iota((STEPS, STEPS), 1)
    allowed_t = (ri >= ci) & ((ri > done) == (ci > done))
    for h in range(HEADS):
        at = slice(h * HD, (h + 1) * HD)
        s = nt(qkv[:, at], qkv[:, D + h * HD : D + (h + 1) * HD]) * SCALE
        s = jnp.where(allowed_t, s, NEG)
        e = jnp.exp(s - jnp.max(s, axis=1, keepdims=True))
        p = (e * (1.0 / jnp.sum(e, axis=1, keepdims=True))).astype(BF16)
        prob_t[h] = p
        mixed[:, at] = nn(p, qkv[:, 2 * D + h * HD : 2 * D + (h + 1) * HD]).astype(BF16)
        if h == V2_AT:
            v_2()
        if h == G2_AT:
            g_2()
    loads[7].wait()
    turn = step_to_block(False)
    for q in range(4):
        at = slice(256 * q, 256 * q + 256)
        h1 = (hid[:, at].astype(F32) + nn(mixed[...], wout[:, at])).astype(BF16)
        for j in range(4):
            stage1[j, q * 64 : q * 64 + 64, :] = h1[j * 64 : j * 64 + 64, :]
    for j in range(4):
        a1[j * 256 : j * 256 + 256, :] = nn(turn, stage1[j]).astype(BF16)

    def block(peer):
        return pl.ds(pl.multiple_of(peer * 16, 16), 16)

    def put_1(peer):
        send(a1.at[block(peer)], r1.at[block(me)], (as1, ar1), 0, {"tm": peer})

    spread(put_1)
    r1[block(me), :] = a1[block(me), :]

    def wait_all(src, dst, sems):
        pltpu.make_async_remote_copy(
            src_ref=src.at[pl.ds(0, 1008)], dst_ref=dst.at[pl.ds(0, 1008)], send_sem=sems[0].at[0],
            recv_sem=sems[1].at[0], device_id=core_id, device_id_type=pl.DeviceIdType.MESH,
        ).wait()

    z_1()
    g_3()
    z_2()
    g_mid()
    wait_all(a1, r1, (as1, ar1))

    unturn = block_to_agent(False)
    for j in range(4):
        got = nn(unturn, r1[j * 256 : j * 256 + 256, :]).astype(BF16)
        for q in range(4):
            for s in range(4):
                i = (q * 4 + s) * 16
                xr[s * 64 + j * 16 : s * 64 + j * 16 + 16, q * 256 : q * 256 + 256] = got[
                    i : i + 16, :
                ]
    xa = xr[...].astype(F32)
    inv_a = lax.rsqrt(jnp.mean(xa * xa, axis=1, keepdims=True) + 1e-6)
    h1_value = jnp.sum(xa * w_value, axis=1, keepdims=True)
    normed = xa * inv_a * gain_a_v[...]
    na[...] = normed.astype(BF16)
    for j in range(4):
        nat[0, j * 256 : j * 256 + 256, :] = normed[:, j * 256 : j * 256 + 256].T.astype(BF16)
    begin("nat", 1, nat.at[0], nat.at[1], G, 29, core_id)
    diag = ri == ci
    alive_f, target_f = alive_v[...].astype(F32), target_v[...]

    def one_row(table):
        return jnp.concatenate([table[s : s + 1, :] for s in range(4)], axis=1)

    def to_column(row):
        return jnp.sum(jnp.where(diag, row, 0.0), axis=1, keepdims=True)

    alive_row = one_row(alive_f)
    alive_col, target_col = to_column(alive_row), to_column(one_row(target_f))
    g_end()

    def project(which):
        for half in range(2):
            for l in range(2):
                at = half * 512 + l * 256
                w = w2[which, half, l].reshape(D, 256)
                qk[which, :, at : at + 256] = nn(na[...], w).astype(BF16)

    project(core)
    finish("gc", 8)
    project(1 - core)
    z_end()
    s_rows = nt(z128[0:32, :], na[...])
    s_rows = s_rows[0:8] + s_rows[16:24]
    square = iota((128, 128), 0), iota((128, 128), 1)
    same_step = (square[0] // 64) == (square[1] // 64)
    sums = []
    for p in range(2):
        rows = slice(128 * p, 128 * p + 128)
        seen = same_step & ((alive_row[:, rows] == 1.0) | (square[0] == square[1]))
        total = jnp.zeros((128, 1), F32)
        for h in range(HEADS):
            at = slice(h * HD, (h + 1) * HD)
            s = nt(qk[0, rows, at], qk[1, rows, at]) * SCALE
            s = jnp.where(seen, s, NEG)
            e = jnp.exp(s - jnp.max(s, axis=1, keepdims=True))
            e = e * (1.0 / jnp.sum(e, axis=1, keepdims=True))
            prob_a[h, p] = e
            total = total + jnp.sum(e * s_rows[h : h + 1, rows], axis=1, keepdims=True)
        sums.append(total)
    predicted = h1_value + jnp.concatenate(sums, axis=0)
    err = 32.0 * alive_col * (predicted - target_col)
    line = jnp.sum(jnp.where(diag, predicted, 0.0), axis=0, keepdims=True)
    for s in range(4):
        values_o[s : s + 1, :] = line[:, s * 64 : s * 64 + 64]
    for p in range(2):
        rows = pl.ds(128 * p, 128)
        for h in range(HEADS):
            at = slice(h * HD, (h + 1) * HD)
            e = prob_a[h, p]
            s_row = s_rows[h : h + 1, 128 * p : 128 * p + 128]
            pv = jnp.sum(e * s_row, axis=1, keepdims=True)
            weighted = e * err[128 * p : 128 * p + 128, :]
            trow[h : h + 1, rows] = jnp.sum(weighted, axis=0, keepdims=True)
            ds = weighted * (s_row - pv) * SCALE
            dqk[0, rows, at] = nn(ds.astype(BF16), qk[1, rows, at]).astype(BF16)
            dqk[1, rows, at] = nn(ds.T.astype(BF16), qk[0, rows, at]).astype(BF16)
        begin("dqk", p + 1, dqk.at[1 - core, rows], dqr.at[rows], G, 30 + p, core_id)

    t_hi = trow[...].astype(BF16).astype(F32)
    t_lo = trow[...] - t_hi
    u_all = nn(jnp.concatenate([t_hi, t_lo], axis=0).astype(BF16), na[...])
    u_all = u_all[0:8] + u_all[8:16]
    for i in range(8):
        for j in range(2):
            at = (j * 4 + i // 2) * 128
            us1[i, j] = u_all[:, at : at + 128]
    for i in range(1, 8):
        begin("uz", i, us1.at[(z + i) % 8], uz.at[i - 1], S, 27 + i, z_peer(i))

    t_all = jnp.concatenate([t_hi, t_lo, t_hi, jnp.zeros((104, STEPS), F32)], axis=0)
    t_col = t_all.T.astype(BF16)
    for i in range(4):
        at = slice(256 * i, 256 * i + 256)
        part = nn(t_col, z128[:, at])
        for c in range(2):
            for half in range(2):
                for l in range(2):
                    w = w2[c, half, l, i // 2, 4 * (i % 2) : 4 * (i % 2) + 4].reshape(256, 256)
                    lanes = half * 512 + l * 256
                    part = part + nt(dqk[c, :, lanes : lanes + 256], w)
        gnorm[:, at] = part * gain_a_v[:, at]

    peers, opp = (y_peer, x_peer), (opp_y, opp_x)

    def term(half, i, zs_):
        if half == 0:
            return tb.at[0, both, both, zs_, rows_of((y + i) % 4)]
        to_h, to_l = x_of(i)
        return tb.at[1, to_l, to_h, zs_]

    def got_1(half, n, zs_):
        return p1y.at[n, both, both, zs_] if half == 0 else p1x.at[n, zs_]

    live[("nat", 1)].wait()
    finish("dqk", 2)
    for half in range(2):
        for l in range(2):
            at = half * 512 + l * 256
            part = nn(nat[0], dqk[core, :, at : at + 256]) + nn(nat[1], dqr[:, at : at + 256])
            tb[half, l] = part.astype(BF16).reshape(2, 8, 64, 256)
        for n, (i, across, plain) in enumerate(((1, first, second), (3, second, first))):
            begin(
                f"q{half}", i, term(half, 2, across), opp[half].at[n], R, 6 * half + n, peers[half](i)
            )
            begin(
                f"p{half}", i, term(half, i, plain), got_1(half, n, plain),
                R, 6 * half + 2 + n, peers[half](i),
            )

    gy = gnorm[...]
    xa = xr[...].astype(F32)
    pull = jnp.mean(xa * gy, axis=1, keepdims=True) * (inv_a * inv_a * inv_a)
    grad = (err * w_value + gy * inv_a - xa * pull).astype(BF16)
    turn = block_to_agent(True)
    for j in range(4):
        for q in range(4):
            for s in range(4):
                i = (q * 4 + s) * 16
                stage2[i : i + 16, j * 256 : j * 256 + 256] = grad[
                    s * 64 + j * 16 : s * 64 + j * 16 + 16, q * 256 : q * 256 + 256
                ]
    for j in range(4):
        a2[j * 256 : j * 256 + 256, :] = nn(turn, stage2[:, j * 256 : j * 256 + 256]).astype(BF16)

    def put_2(peer):
        send(a2.at[block(peer)], r2.at[block(me)], (as2, ar2), 0, {"tm": peer})

    spread(put_2)
    r2[block(me), :] = a2[block(me), :]

    def u_xy():
        finish("uz", 7)
        um[...] = us1[z] + jnp.sum(uz[...], axis=0)
        for i in range(1, 8):
            begin("uxy", i, um.at[xy_of(i)[0]], uxy.at[i - 1], S, 34 + i, xy_peer(i))

    def u_env():
        finish("uxy", 7)
        uf[...] = um[xh] + jnp.sum(uxy[...], axis=0)
        for i in (1, 2, 3):
            begin("ue", i, uf, ue.at[i - 1], S, 41 + i, {"env": (env + i) % 4})

    def u_mix():
        finish("ue", 3)
        u = uf[...] + jnp.sum(ue[...], axis=0)
        v8 = jnp.sum(vb2[...], axis=0)
        lines = []
        for h in range(HEADS):
            at = slice(2 * D + h * HD, 2 * D + (h + 1) * HD)
            col = jnp.sum(jnp.where(spot, u[h : h + 1, :], 0.0), axis=1, keepdims=True)
            qkvg_o[:, at] = col * v8[h : h + 1, :]
            lines.append(jnp.sum(col * wqkva_v[:, at].astype(F32), axis=0, keepdims=True))
        up[...] = jnp.concatenate(lines, axis=0)
        for i in range(1, 8):
            begin("uq", i, up, uq.at[i - 1], S, 44 + i, z_peer(i))

    def u_last():
        finish("uq", 7)
        uw[...] = up[...] + jnp.sum(uq[...], axis=0)
        for i in range(1, 8):
            begin("ux", i, uw, ux.at[i - 1], S, 51 + i, xy_peer(i))

    def u_end():
        finish("ux", 7)
        total = uw[...] + jnp.sum(ux[...], axis=0)
        row = jnp.sum(jnp.where(own_line, total, 0.0), axis=0, keepdims=True)
        outg_o[...] = jnp.sum(jnp.where(spot, row, 0.0), axis=1, keepdims=True) * w_value

    def r_1():
        for half in range(2):
            for n, (i, across) in enumerate(((1, first), (3, second))):
                live[(f"q{half}", i)].wait()
                z0 = 4 * n
                if half == 0:
                    rows = rows_of((y + i) % 4)
                    for l in range(2):
                        for k in range(2):
                            both_terms = tb[0, l, k, z0 : z0 + 4, rows, :] + opp_y[n, l, k]
                            tb[0, l, k, z0 : z0 + 4, rows, :] = both_terms
                else:
                    to_h, to_l = x_of(i)
                    for k in range(4):
                        tb[1, to_l, to_h, z0 + k] = tb[1, to_l, to_h, z0 + k] + opp_x[n, k]
                begin(
                    f"r{half}", i, term(half, i, across), got_1(half, n, across),
                    R, 6 * half + 4 + n, peers[half](i),
                )

    def r_2():
        for name in ("p0", "r0"):
            for i in (1, 3):
                live[(name, i)].wait()
        for l in range(2):
            for i in range(2):
                total = tb[0, l, i, :, own_rows, :].astype(F32)
                for k in range(2):
                    total = total + p1y[k, l, i].astype(F32)
                s1[l, i] = total.astype(BF16)
        for i in (1, 2, 3):
            to_h, to_l = x_of(i)
            begin("p2x", i, s1.at[to_l, to_h], p2x.at[i - 1], R, 11 + i, x_peer(i))
        for name in ("p1", "r1"):
            for i in (1, 3):
                live[(name, i)].wait()
        for i in range(8):
            total = tb[1, xl, xh, i].astype(F32)
            for k in range(2):
                total = total + p1x[k, i].astype(F32)
            s2[i] = total.astype(BF16)
        for i in (1, 2, 3):
            begin(
                "p2y", i, s2.at[every, rows_of((y + i) % 4)], p2y.at[i - 1], R, 14 + i, y_peer(i)
            )

    def r_z():
        finish("p2x", 3)
        total = s1[xl, xh].astype(F32)
        for k in range(3):
            total = total + p2x[k].astype(F32)
        s3[0] = total.astype(BF16)
        finish("p2y", 3)
        total = s2[:, own_rows, :].astype(F32)
        for k in range(3):
            total = total + p2y[k].astype(F32)
        s3[1] = total.astype(BF16)
        for i in range(1, 8):
            begin("pz", i, s3.at[both, (z + i) % 8], pz.at[i - 1], R, 17 + i, z_peer(i))

    def r_env():
        finish("pz", 7)
        total = s3[:, z].astype(F32)
        for k in range(7):
            total = total + pz[k].astype(F32)
        eb[env] = total
        for i in (1, 2, 3):
            begin("eb", i, eb.at[env], eb.at[env], R, 24 + i, {"env": (env + i) % 4})

    def r_end():
        finish("eb", 3)
        for e in range(4):
            for half in range(2):
                at = (e % 2) * D + half * 512 + (e // 2) * 256
                qkvg_o[:, at : at + 256] = eb[e, half]

    r_1()
    u_xy()
    r_2()
    u_env()

    wait_all(a2, r2, (as2, ar2))
    unturn = step_to_block(True)
    for j in range(4):
        got = nn(unturn, r2[j * 256 : j * 256 + 256, :]).astype(BF16)
        for q in range(4):
            gh[j * 64 : j * 64 + 64, q * 256 : q * 256 + 256] = got[q * 64 : q * 64 + 64, :]
    after = {1: r_z, 2: u_mix, 5: u_last}
    for h in range(HEADS):
        at = slice(h * HD, (h + 1) * HD)
        at_k, at_v = slice(D + h * HD, D + (h + 1) * HD), slice(2 * D + h * HD, 2 * D + (h + 1) * HD)
        gm = nt(gh[...], wout[at, :]).astype(BF16)
        p = prob_t[h]
        pf = p.astype(F32)
        dp = nt(gm, qkv[:, at_v])
        ds = (pf * (dp - jnp.sum(pf * dp, axis=1, keepdims=True)) * SCALE)
        q_h, k_h = qkv[:, at], qkv[:, at_k]
        qkv[:, at_v] = nn(pf.T.astype(BF16), gm).astype(BF16)
        qkv[:, at] = nn(ds.astype(BF16), k_h).astype(BF16)
        qkv[:, at_k] = nn(ds.T.astype(BF16), q_h).astype(BF16)
        if h in after:
            after[h]()
    r_env()
    for i in range(4):
        at = slice(256 * i, 256 * i + 256)
        gnorm[:, at] = nt(qkv[...], wqkv[at, :]) * gain_t_v[:, at]
    gy = gnorm[...]
    x = hid[...].astype(F32)
    inv_t = lax.rsqrt(jnp.mean(x * x, axis=1, keepdims=True) + 1e-6)
    pull = jnp.mean(x * gy, axis=1, keepdims=True) * (inv_t * inv_t * inv_t)
    igrad_o[...] = (gh[...].astype(F32) + gy * inv_t - x * pull).astype(BF16)
    u_end()
    r_end()


def hand_on(*refs):
    for i in range(4):
        refs[4 + i][...] = refs[i][...]


def per_device(
    hidden, done_step, alive, targets, gain_t, w_qkv_t, w_out_t, gain_a, w_qkv_a, w_out_a, w_value
):
    vmem = pl.BlockSpec(memory_space=pltpu.VMEM)
    away = pl.BlockSpec(memory_space=pl.ANY)
    mem = pltpu.VMEM
    dma = pltpu.SemaphoreType.DMA
    tile = (8, 128)
    scratch = [
        mem((STEPS, D), BF16), mem((D, 3 * D), BF16), mem((D, D), BF16), mem((STEPS, D), BF16),
        mem((STEPS, 3 * D), BF16), mem((HEADS, STEPS, STEPS), BF16), mem((STEPS, D), BF16),
        mem((4, 256, 256), BF16), mem((1024, 256), BF16), mem((1024, 256), BF16),
        mem((STEPS, D), BF16),
        mem((2, 2, 2, 2, 8, 64, 256), BF16), mem((8, *tile), F32), mem((8, *tile), F32),
        mem((2, 4, *tile), F32), mem((8, 2, *tile), F32), mem((128, D), BF16),
        mem((STEPS, D), BF16), mem((2, D, STEPS), BF16), mem((2, STEPS, D), BF16),
        mem((HEADS, 2, 128, 128), F32), mem((2, STEPS, D), BF16), mem((STEPS, D), BF16),
        mem((HEADS, STEPS), F32), mem((STEPS, D), F32), mem((256, 1024), BF16),
        mem((1024, 256), BF16), mem((1024, 256), BF16), mem((STEPS, D), BF16),
        mem((2, 2, 2, 8, 64, 256), BF16), mem((2, 2, 2, 4, 16, 256), BF16),
        mem((2, 4, 64, 256), BF16), mem((2, 2, 2, 8, 16, 256), BF16), mem((2, 8, 64, 256), BF16), mem((2, 2, 8, 16, 256), BF16), mem((8, 64, 256), BF16),
        mem((3, 8, 16, 256), BF16), mem((3, 8, 16, 256), BF16), mem((2, 8, 16, 256), BF16),
        mem((7, 2, 16, 256), BF16), mem((4, 2, 16, 256), F32),
        mem((8, 2, *tile), F32), mem((7, 2, *tile), F32), mem((2, *tile), F32),
        mem((7, *tile), F32), mem(tile, F32), mem((3, *tile), F32), mem(tile, F32),
        mem((7, *tile), F32), mem(tile, F32), mem((7, *tile), F32),
        dma((8,)), dma((32,)), dma((32,)), dma((1,)), dma((1,)), dma((1,)), dma((1,)),
        dma((59,)), dma((59,)), dma((28,)), dma((28,)),
    ]
    shapes = (
            jax.ShapeDtypeStruct((4, AGENTS), F32),
            jax.ShapeDtypeStruct((STEPS, D), BF16),
            jax.ShapeDtypeStruct((16, 3 * D), F32),
            jax.ShapeDtypeStruct((16, D), F32),
    )
    results = pl.pallas_call(
        kernel,
        out_shape=shapes,
        in_specs=[away, vmem, vmem, vmem, vmem, away, away, vmem, vmem, vmem, vmem],
        out_specs=(vmem, vmem, vmem, vmem),
        scratch_shapes=scratch,
        compiler_params=pltpu.CompilerParams(
            collective_id=0, has_side_effects=True, vmem_limit_bytes=60 * 2**20
        ),
    )(
        hidden[0, 0], done_step, alive[0].T, targets[0].T, gain_t[None], w_qkv_t, w_out_t, gain_a[None], w_qkv_a,
        w_out_a, w_value[None],
    )
    values, input_grad, qkv_grad, out_grad = pl.pallas_call(
        hand_on, out_shape=shapes, in_specs=[vmem] * 4, out_specs=(vmem,) * 4
    )(*results)
    return values.T[None], input_grad[None, None], qkv_grad, out_grad


def solution(mesh):
    in_specs = (
        P("env", "tm", None, None),
        P("env", "tm"),
        P("env", None, "tm"),
        P("env", None, "tm"),
        P(),
        P(),
        P(),
        P(),
        P("tm", None),
        P("tm", None),
        P(),
    )
    out_specs = (P("env", None, "tm"), P("env", "tm", None, None), P("tm", None), P("tm", None))
    return jax.shard_map(
        per_device, mesh=mesh, in_specs=in_specs, out_specs=out_specs, check_vma=False
    )
```

```python
import math

import jax
import jax.numpy as jnp
from jax import lax
from jax.experimental import pallas as pl
from jax.experimental.pallas import tpu as pltpu
from jax.sharding import PartitionSpec as P

F32, BF16 = jnp.float32, jnp.bfloat16
HEADS, D, STEPS, AGENTS = 8, 1024, 256, 64
HD = D // HEADS
SCALE = 1.0 / math.sqrt(HD)
NEG = -1e30
BAR, V2_AT, G2_AT = 4, 2, 7


def dot(a, b, ca, cb):
    return lax.dot_general(a, b, (((ca,), (cb,)), ((), ())), preferred_element_type=F32)


def nn(a, b):
    return dot(a, b, 1, 0)


def nt(a, b):
    return dot(a, b, 1, 1)


def tn(a, b):
    return dot(a, b, 0, 0)


def iota(shape, axis):
    return lax.broadcasted_iota(jnp.int32, shape, axis)


def split(x):
    high = x.astype(BF16)
    return high, (x - high.astype(F32)).astype(BF16)


def pick(condition):
    return jnp.where(condition, 1.0, 0.0).astype(BF16)


def step_to_block(flip):
    i, c = iota((256, 256), 1 if flip else 0), iota((256, 256), 0 if flip else 1)
    return pick(((i // 4) % 4 == c // 64) & (c % 64 == (i // 16) * 4 + i % 4))


def block_to_agent(flip):
    i, c = iota((256, 256), 1 if flip else 0), iota((256, 256), 0 if flip else 1)
    return pick((i % 16 == c // 16) & (i // 16 == c % 16))


def kernel(
    hidden_h, done_v, alive_v, target_v, gain_t_v, wqkv_h, wout_h, gain_a_v, wqkva_v, wouta_v, wval_v,
    values_o, igrad_o, qkvg_o, outg_o,
    hid, wqkv, wout, norm_t, qkv, prob_t, mixed, stage1, a1, r1, xr,
    w2, vb1, vb2, zb1, zb2, z128, na, nat, qk, prob_a, dqk, dqr, trow, gnorm, stage2, a2, r2, gh,
    tb, opp_y, opp_x, p1y, p1x, s1, s2, p2x, p2y, s3, pz, eb, us1, uz, um, uxy, uf, ue, up, uq, uw, ux,
    lsem, gs, gr, as1, ar1, as2, ar2, ss, sr, rs, rr,
):
    me, env = lax.axis_index("tm"), lax.axis_index("env")
    core, xl = env % 2, env // 2
    xh, z, y = me // 32, (me // 4) % 8, me % 4
    x_at = xh * 2 + xl
    core_id = {"env": env + 1 - 2 * core}

    def tm_at(xh_, z_, y_):
        return {"tm": xh_ * 32 + z_ * 4 + y_}

    def x_of(i):
        to = (x_at + i) % 4
        return to // 2, to % 2

    def x_peer(i):
        to_h, to_l = x_of(i)
        return {"env": to_l * 2 + core, "tm": to_h * 32 + z * 4 + y}

    def y_peer(i):
        return tm_at(xh, z, (y + i) % 4)

    def z_peer(i):
        return tm_at(xh, (z + i) % 8, y)

    def xy_of(i):
        to = (xh * 4 + y + i) % 8
        return to // 4, to % 4

    def xy_peer(i):
        to_h, to_y = xy_of(i)
        return tm_at(to_h, z, to_y)

    def send(src, dst, sems, k, where):
        copy = pltpu.make_async_remote_copy(
            src_ref=src, dst_ref=dst, send_sem=sems[0].at[k], recv_sem=sems[1].at[k],
            device_id=where, device_id_type=pl.DeviceIdType.MESH,
        )
        copy.start()
        return copy

    def spread(body):
        def step(i, carry):
            body(lax.rem(me + i, 64))
            return carry
        lax.fori_loop(1, 64, step, 0)

    barrier = pltpu.get_barrier_semaphore()

    def greet(where):
        pl.semaphore_signal(
            barrier, inc=1, device_id=where, device_id_type=pl.DeviceIdType.MESH
        )

    for i in range(1, 8):
        greet(z_peer(i))
    for i in range(1, 8):
        greet(xy_peer(i))
    greet({"env": (env + 2) % 4, "tm": (1 - xh) * 32 + z * 4 + y})
    for i in (1, 2, 3):
        greet({"env": (env + i) % 4})

    loads = [pltpu.make_async_copy(hidden_h, hid, lsem.at[0])]
    for j in range(6):
        at = (slice(None), slice(512 * j, 512 * j + 512))
        loads.append(pltpu.make_async_copy(wqkv_h.at[at], wqkv.at[at], lsem.at[1 + j]))
    loads.append(pltpu.make_async_copy(wout_h, wout, lsem.at[7]))
    for load in loads:
        load.start()

    w_value = wval_v[...]
    lane_off = (me % 8) * 16
    spot = iota((16, 128), 1) == iota((16, 128), 0) + lane_off
    own_line = iota((8, 128), 0) == me // 8

    def to_lanes(column):
        return jnp.sum(jnp.where(spot, column, 0.0), axis=0, keepdims=True)

    def rows_of(y_):
        return pl.ds(pl.multiple_of(y_ * 16, 16), 16)

    own_rows = rows_of(y)
    for half in range(2):
        at = pl.multiple_of(core * D + half * 512 + xl * 256, 256)
        w2[core, half, xl, xh, z, own_rows, :] = wqkva_v[:, pl.ds(at, 256)]
    v_part = jnp.sum(wouta_v[...].astype(F32) * w_value, axis=1, keepdims=True)
    vb1[0] = jnp.where(own_line, to_lanes(v_part), 0.0)

    G, S, R = (gs, gr), (ss, sr), (rs, rr)
    both, every = pl.ds(0, 2), pl.ds(0, 8)
    live = {}

    def begin(name, i, *what):
        live[(name, i)] = send(*what)

    def finish(name, n):
        for i in range(1, n + 1):
            live[(name, i)].wait()

    def g_z():
        ref = w2.at[core, both, xl, xh, z, own_rows]
        for i in range(1, 8):
            begin("gz", i, ref, ref, G, i - 1, z_peer(i))

    def g_2():
        finish("gz", 7)
        for i in (1, 2, 3):
            for half, peer, k in ((0, x_peer(i), 6), (1, y_peer(i), 9)):
                ref = w2.at[core, half, xl, xh, every, own_rows]
                begin(f"g2{half}", i, ref, ref, G, k + i, peer)

    def to_core(k, ref):
        begin("gc", k + 1, ref, ref, G, 21 + k, core_id)

    first, second = pl.ds(0, 4), pl.ds(4, 4)

    def y_piece(i, zs_=every):
        return w2.at[core, 0, both, both, zs_, rows_of((y + i) % 4)]

    def x_piece(i, zs_=every):
        to_h, to_l = x_of(i)
        return w2.at[core, 1, to_l, to_h, zs_]

    def g_3():
        for half, part, peer in ((0, y_piece, y_peer), (1, x_piece, x_peer)):
            finish(f"g2{half}", 3)
            for i in (1, 3):
                begin(f"g3{half}", i, part(0), part(0), G, 13 + 4 * half + i // 2, peer(i))
            to_core(4 * half, part(0))

    def g_mid():
        for half, part, peer in ((0, y_piece, y_peer), (1, x_piece, x_peer)):
            for i, zs_ in ((1, first), (3, second)):
                live[(f"g3{half}", i)].wait()
                ref = part(4 - i, zs_)
                begin(f"g4{half}", i, ref, ref, G, 15 + 4 * half + i // 2, peer(i))
        for half, part in ((0, y_piece), (1, x_piece)):
            for i in (1, 3):
                to_core(4 * half + 1 + i // 2, part(4 - i))

    def g_end():
        for half, part in ((0, y_piece), (1, x_piece)):
            for i in (1, 3):
                live[(f"g4{half}", i)].wait()
            to_core(4 * half + 3, part(2))

    def v_1():
        for i in range(1, 8):
            begin("v1", i, vb1.at[0], vb1.at[i], S, i - 1, xy_peer(i))

    def v_2():
        finish("v1", 7)
        vb2[0] = jnp.sum(vb1[...], axis=0)
        for i in range(1, 8):
            begin("v2", i, vb2.at[0], vb2.at[i], S, 6 + i, z_peer(i))

    def z_1():
        finish("v2", 7)
        v8 = jnp.sum(vb2[...], axis=0)
        rows = []
        for h in range(HEADS):
            w_v = wqkva_v[:, 2 * D + h * HD : 2 * D + (h + 1) * HD].astype(F32)
            col = jnp.sum(w_v * v8[h : h + 1, :], axis=1, keepdims=True)
            rows.append(to_lanes(col))
        zb1[xh, y] = jnp.concatenate(rows, axis=0)
        for i in range(1, 8):
            begin("z1", i, zb1.at[xh, y], zb1.at[xh, y], S, 13 + i, xy_peer(i))

    def z_2():
        finish("z1", 7)
        zb2[z] = jnp.sum(zb1[...], axis=1)
        for i in range(1, 8):
            begin("z2", i, zb2.at[z], zb2.at[z], S, 20 + i, z_peer(i))

    def z_end():
        finish("z2", 7)
        tiles = []
        for i in range(2):
            for j in range(4):
                tiles.append(zb2[2 * j, i] + zb2[2 * j + 1, i])
        z_hi, z_lo = split(jnp.concatenate(tiles, axis=1))
        z128[...] = jnp.zeros((128, D), BF16)
        z128[0:16, :] = jnp.concatenate([z_hi, z_hi], axis=0)
        z128[16:32, :] = jnp.concatenate([z_lo, jnp.zeros_like(z_lo)], axis=0)

    loads[0].wait()
    x = hid[...].astype(F32)
    inv_t = lax.rsqrt(jnp.mean(x * x, axis=1, keepdims=True) + 1e-6)
    norm_t[...] = (x * inv_t * gain_t_v[...]).astype(BF16)
    for j in range(6):
        loads[1 + j].wait()
        at = slice(512 * j, 512 * j + 512)
        qkv[:, at] = nn(norm_t[...], wqkv[:, at]).astype(BF16)
        if j == BAR:
            pl.semaphore_wait(barrier, 18)
            g_z()
            v_1()
    done = done_v[...]
    ri, ci = iota((STEPS, STEPS), 0), iota((STEPS, STEPS), 1)
    allowed_t = (ri >= ci) & ((ri > done) == (ci > done))
    for h in range(HEADS):
        at = slice(h * HD, (h + 1) * HD)
        s = nt(qkv[:, at], qkv[:, D + h * HD : D + (h + 1) * HD]) * SCALE
        s = jnp.where(allowed_t, s, NEG)
        e = jnp.exp(s - jnp.max(s, axis=1, keepdims=True))
        p = (e * (1.0 / jnp.sum(e, axis=1, keepdims=True))).astype(BF16)
        prob_t[h] = p
        mixed[:, at] = nn(p, qkv[:, 2 * D + h * HD : 2 * D + (h + 1) * HD]).astype(BF16)
        if h == V2_AT:
            v_2()
        if h == G2_AT:
            g_2()
    loads[7].wait()
    turn = step_to_block(False)
    for q in range(4):
        at = slice(256 * q, 256 * q + 256)
        h1 = (hid[:, at].astype(F32) + nn(mixed[...], wout[:, at])).astype(BF16)
        for j in range(4):
            stage1[j, q * 64 : q * 64 + 64, :] = h1[j * 64 : j * 64 + 64, :]
    for j in range(4):
        a1[j * 256 : j * 256 + 256, :] = nn(turn, stage1[j]).astype(BF16)

    def block(peer):
        return pl.ds(pl.multiple_of(peer * 16, 16), 16)

    def put_1(peer):
        send(a1.at[block(peer)], r1.at[block(me)], (as1, ar1), 0, {"tm": peer})

    spread(put_1)
    r1[block(me), :] = a1[block(me), :]

    def wait_all(src, dst, sems):
        pltpu.make_async_remote_copy(
            src_ref=src.at[pl.ds(0, 1008)], dst_ref=dst.at[pl.ds(0, 1008)], send_sem=sems[0].at[0],
            recv_sem=sems[1].at[0], device_id=core_id, device_id_type=pl.DeviceIdType.MESH,
        ).wait()

    z_1()
    g_3()
    g_mid()
    z_2()
    wait_all(a1, r1, (as1, ar1))

    unturn = block_to_agent(False)
    for j in range(4):
        got = nn(unturn, r1[j * 256 : j * 256 + 256, :]).astype(BF16)
        for q in range(4):
            for s in range(4):
                i = (q * 4 + s) * 16
                xr[s * 64 + j * 16 : s * 64 + j * 16 + 16, q * 256 : q * 256 + 256] = got[
                    i : i + 16, :
                ]
    xa = xr[...].astype(F32)
    inv_a = lax.rsqrt(jnp.mean(xa * xa, axis=1, keepdims=True) + 1e-6)
    h1_value = jnp.sum(xa * w_value, axis=1, keepdims=True)
    normed = xa * inv_a * gain_a_v[...]
    na[...] = normed.astype(BF16)
    for j in range(4):
        nat[0, j * 256 : j * 256 + 256, :] = normed[:, j * 256 : j * 256 + 256].T.astype(BF16)
    begin("nat", 1, nat.at[0], nat.at[1], G, 29, core_id)
    diag = ri == ci
    alive_f, target_f = alive_v[...].astype(F32), target_v[...]

    def one_row(table):
        return jnp.concatenate([table[s : s + 1, :] for s in range(4)], axis=1)

    def to_column(row):
        return jnp.sum(jnp.where(diag, row, 0.0), axis=1, keepdims=True)

    alive_row = one_row(alive_f)
    alive_col, target_col = to_column(alive_row), to_column(one_row(target_f))
    g_end()

    def project(which):
        for half in range(2):
            for l in range(2):
                at = half * 512 + l * 256
                w = w2[which, half, l].reshape(D, 256)
                qk[which, :, at : at + 256] = nn(na[...], w).astype(BF16)

    project(core)
    finish("gc", 8)
    project(1 - core)
    z_end()
    s_rows = nt(z128[0:32, :], na[...])
    s_rows = s_rows[0:8] + s_rows[16:24]
    square = iota((128, 128), 0), iota((128, 128), 1)
    same_step = (square[0] // 64) == (square[1] // 64)
    sums = []
    for p in range(2):
        rows = slice(128 * p, 128 * p + 128)
        seen = same_step & ((alive_row[:, rows] == 1.0) | (square[0] == square[1]))
        total = jnp.zeros((128, 1), F32)
        for h in range(HEADS):
            at = slice(h * HD, (h + 1) * HD)
            s = nt(qk[0, rows, at], qk[1, rows, at]) * SCALE
            s = jnp.where(seen, s, NEG)
            e = jnp.exp(s - jnp.max(s, axis=1, keepdims=True))
            e = e * (1.0 / jnp.sum(e, axis=1, keepdims=True))
            prob_a[h, p] = e
            total = total + jnp.sum(e * s_rows[h : h + 1, rows], axis=1, keepdims=True)
        sums.append(total)
    predicted = h1_value + jnp.concatenate(sums, axis=0)
    err = 32.0 * alive_col * (predicted - target_col)
    line = jnp.sum(jnp.where(diag, predicted, 0.0), axis=0, keepdims=True)
    for s in range(4):
        values_o[s : s + 1, :] = line[:, s * 64 : s * 64 + 64]
    for p in range(2):
        rows = pl.ds(128 * p, 128)
        for h in range(HEADS):
            at = slice(h * HD, (h + 1) * HD)
            e = prob_a[h, p]
            s_row = s_rows[h : h + 1, 128 * p : 128 * p + 128]
            pv = jnp.sum(e * s_row, axis=1, keepdims=True)
            weighted = e * err[128 * p : 128 * p + 128, :]
            trow[h : h + 1, rows] = jnp.sum(weighted, axis=0, keepdims=True)
            ds = weighted * (s_row - pv) * SCALE
            dqk[0, rows, at] = nn(ds.astype(BF16), qk[1, rows, at]).astype(BF16)
            dqk[1, rows, at] = nn(ds.T.astype(BF16), qk[0, rows, at]).astype(BF16)
        begin("dqk", p + 1, dqk.at[1 - core, rows], dqr.at[rows], G, 30 + p, core_id)

    t_hi = trow[...].astype(BF16).astype(F32)
    t_lo = trow[...] - t_hi
    u_all = nn(jnp.concatenate([t_hi, t_lo], axis=0).astype(BF16), na[...])
    u_all = u_all[0:8] + u_all[8:16]
    for i in range(8):
        for j in range(2):
            at = (j * 4 + i // 2) * 128
            us1[i, j] = u_all[:, at : at + 128]
    for i in range(1, 8):
        begin("uz", i, us1.at[(z + i) % 8], uz.at[i - 1], S, 27 + i, z_peer(i))

    t_all = jnp.concatenate([t_hi, t_lo, t_hi, jnp.zeros((104, STEPS), F32)], axis=0)
    t_col = t_all.T.astype(BF16)
    for i in range(4):
        at = slice(256 * i, 256 * i + 256)
        part = nn(t_col, z128[:, at])
        for c in range(2):
            for half in range(2):
                for l in range(2):
                    w = w2[c, half, l, i // 2, 4 * (i % 2) : 4 * (i % 2) + 4].reshape(256, 256)
                    lanes = half * 512 + l * 256
                    part = part + nt(dqk[c, :, lanes : lanes + 256], w)
        gnorm[:, at] = part * gain_a_v[:, at]

    peers, opp = (y_peer, x_peer), (opp_y, opp_x)

    def term(half, i, zs_):
        if half == 0:
            return tb.at[0, both, both, zs_, rows_of((y + i) % 4)]
        to_h, to_l = x_of(i)
        return tb.at[1, to_l, to_h, zs_]

    def got_1(half, n, zs_):
        return p1y.at[n, both, both, zs_] if half == 0 else p1x.at[n, zs_]

    live[("nat", 1)].wait()
    finish("dqk", 2)
    for half in range(2):
        for l in range(2):
            at = half * 512 + l * 256
            part = nn(nat[0], dqk[core, :, at : at + 256]) + nn(nat[1], dqr[:, at : at + 256])
            tb[half, l] = part.astype(BF16).reshape(2, 8, 64, 256)
        for n, (i, across, plain) in enumerate(((1, first, second), (3, second, first))):
            begin(
                f"q{half}", i, term(half, 2, across), opp[half].at[n], R, 6 * half + n, peers[half](i)
            )
            begin(
                f"p{half}", i, term(half, i, plain), got_1(half, n, plain),
                R, 6 * half + 2 + n, peers[half](i),
            )

    gy = gnorm[...]
    xa = xr[...].astype(F32)
    pull = jnp.mean(xa * gy, axis=1, keepdims=True) * (inv_a * inv_a * inv_a)
    grad = (err * w_value + gy * inv_a - xa * pull).astype(BF16)
    turn = block_to_agent(True)
    for j in range(4):
        for q in range(4):
            for s in range(4):
                i = (q * 4 + s) * 16
                stage2[i : i + 16, j * 256 : j * 256 + 256] = grad[
                    s * 64 + j * 16 : s * 64 + j * 16 + 16, q * 256 : q * 256 + 256
                ]
    for j in range(4):
        a2[j * 256 : j * 256 + 256, :] = nn(turn, stage2[:, j * 256 : j * 256 + 256]).astype(BF16)

    def put_2(peer):
        send(a2.at[block(peer)], r2.at[block(me)], (as2, ar2), 0, {"tm": peer})

    spread(put_2)
    r2[block(me), :] = a2[block(me), :]

    def u_xy():
        finish("uz", 7)
        um[...] = us1[z] + jnp.sum(uz[...], axis=0)
        for i in range(1, 8):
            begin("uxy", i, um.at[xy_of(i)[0]], uxy.at[i - 1], S, 34 + i, xy_peer(i))

    def u_env():
        finish("uxy", 7)
        uf[...] = um[xh] + jnp.sum(uxy[...], axis=0)
        for i in (1, 2, 3):
            begin("ue", i, uf, ue.at[i - 1], S, 41 + i, {"env": (env + i) % 4})

    def u_mix():
        finish("ue", 3)
        u = uf[...] + jnp.sum(ue[...], axis=0)
        v8 = jnp.sum(vb2[...], axis=0)
        lines = []
        for h in range(HEADS):
            at = slice(2 * D + h * HD, 2 * D + (h + 1) * HD)
            col = jnp.sum(jnp.where(spot, u[h : h + 1, :], 0.0), axis=1, keepdims=True)
            qkvg_o[:, at] = col * v8[h : h + 1, :]
            lines.append(jnp.sum(col * wqkva_v[:, at].astype(F32), axis=0, keepdims=True))
        up[...] = jnp.concatenate(lines, axis=0)
        for i in range(1, 8):
            begin("uq", i, up, uq.at[i - 1], S, 44 + i, z_peer(i))

    def u_last():
        finish("uq", 7)
        uw[...] = up[...] + jnp.sum(uq[...], axis=0)
        for i in range(1, 8):
            begin("ux", i, uw, ux.at[i - 1], S, 51 + i, xy_peer(i))

    def u_end():
        finish("ux", 7)
        total = uw[...] + jnp.sum(ux[...], axis=0)
        row = jnp.sum(jnp.where(own_line, total, 0.0), axis=0, keepdims=True)
        outg_o[...] = jnp.sum(jnp.where(spot, row, 0.0), axis=1, keepdims=True) * w_value

    def r_1():
        for half in range(2):
            for n, (i, across) in enumerate(((1, first), (3, second))):
                live[(f"q{half}", i)].wait()
                z0 = 4 * n
                if half == 0:
                    rows = rows_of((y + i) % 4)
                    for l in range(2):
                        for k in range(2):
                            both_terms = tb[0, l, k, z0 : z0 + 4, rows, :] + opp_y[n, l, k]
                            tb[0, l, k, z0 : z0 + 4, rows, :] = both_terms
                else:
                    to_h, to_l = x_of(i)
                    for k in range(4):
                        tb[1, to_l, to_h, z0 + k] = tb[1, to_l, to_h, z0 + k] + opp_x[n, k]
                begin(
                    f"r{half}", i, term(half, i, across), got_1(half, n, across),
                    R, 6 * half + 4 + n, peers[half](i),
                )

    def r_2():
        for name in ("p0", "r0"):
            for i in (1, 3):
                live[(name, i)].wait()
        for l in range(2):
            for i in range(2):
                total = tb[0, l, i, :, own_rows, :].astype(F32)
                for k in range(2):
                    total = total + p1y[k, l, i].astype(F32)
                s1[l, i] = total.astype(BF16)
        for i in (1, 2, 3):
            to_h, to_l = x_of(i)
            begin("p2x", i, s1.at[to_l, to_h], p2x.at[i - 1], R, 11 + i, x_peer(i))
        for name in ("p1", "r1"):
            for i in (1, 3):
                live[(name, i)].wait()
        for i in range(8):
            total = tb[1, xl, xh, i].astype(F32)
            for k in range(2):
                total = total + p1x[k, i].astype(F32)
            s2[i] = total.astype(BF16)
        for i in (1, 2, 3):
            begin(
                "p2y", i, s2.at[every, rows_of((y + i) % 4)], p2y.at[i - 1], R, 14 + i, y_peer(i)
            )

    def r_z():
        finish("p2x", 3)
        total = s1[xl, xh].astype(F32)
        for k in range(3):
            total = total + p2x[k].astype(F32)
        s3[0] = total.astype(BF16)
        finish("p2y", 3)
        total = s2[:, own_rows, :].astype(F32)
        for k in range(3):
            total = total + p2y[k].astype(F32)
        s3[1] = total.astype(BF16)
        for i in range(1, 8):
            begin("pz", i, s3.at[both, (z + i) % 8], pz.at[i - 1], R, 17 + i, z_peer(i))

    def r_env():
        finish("pz", 7)
        total = s3[:, z].astype(F32)
        for k in range(7):
            total = total + pz[k].astype(F32)
        eb[env] = total
        for i in (1, 2, 3):
            begin("eb", i, eb.at[env], eb.at[env], R, 24 + i, {"env": (env + i) % 4})

    def r_end():
        finish("eb", 3)
        for e in range(4):
            for half in range(2):
                at = (e % 2) * D + half * 512 + (e // 2) * 256
                qkvg_o[:, at : at + 256] = eb[e, half]

    r_1()
    u_xy()
    r_2()
    u_env()

    wait_all(a2, r2, (as2, ar2))
    unturn = step_to_block(True)
    for j in range(4):
        got = nn(unturn, r2[j * 256 : j * 256 + 256, :]).astype(BF16)
        for q in range(4):
            gh[j * 64 : j * 64 + 64, q * 256 : q * 256 + 256] = got[q * 64 : q * 64 + 64, :]
    after = {1: r_z, 2: u_mix, 5: u_last}
    for h in range(HEADS):
        at = slice(h * HD, (h + 1) * HD)
        at_k, at_v = slice(D + h * HD, D + (h + 1) * HD), slice(2 * D + h * HD, 2 * D + (h + 1) * HD)
        gm = nt(gh[...], wout[at, :]).astype(BF16)
        p = prob_t[h]
        pf = p.astype(F32)
        dp = nt(gm, qkv[:, at_v])
        ds = (pf * (dp - jnp.sum(pf * dp, axis=1, keepdims=True)) * SCALE)
        q_h, k_h = qkv[:, at], qkv[:, at_k]
        qkv[:, at_v] = nn(pf.T.astype(BF16), gm).astype(BF16)
        qkv[:, at] = nn(ds.astype(BF16), k_h).astype(BF16)
        qkv[:, at_k] = nn(ds.T.astype(BF16), q_h).astype(BF16)
        if h in after:
            after[h]()
    r_env()
    for i in range(4):
        at = slice(256 * i, 256 * i + 256)
        gnorm[:, at] = nt(qkv[...], wqkv[at, :]) * gain_t_v[:, at]
    gy = gnorm[...]
    x = hid[...].astype(F32)
    inv_t = lax.rsqrt(jnp.mean(x * x, axis=1, keepdims=True) + 1e-6)
    pull = jnp.mean(x * gy, axis=1, keepdims=True) * (inv_t * inv_t * inv_t)
    igrad_o[...] = (gh[...].astype(F32) + gy * inv_t - x * pull).astype(BF16)
    u_end()
    r_end()


def hand_on(*refs):
    for i in range(4):
        refs[4 + i][...] = refs[i][...]


def per_device(
    hidden, done_step, alive, targets, gain_t, w_qkv_t, w_out_t, gain_a, w_qkv_a, w_out_a, w_value
):
    vmem = pl.BlockSpec(memory_space=pltpu.VMEM)
    away = pl.BlockSpec(memory_space=pl.ANY)
    mem = pltpu.VMEM
    dma = pltpu.SemaphoreType.DMA
    tile = (8, 128)
    scratch = [
        mem((STEPS, D), BF16), mem((D, 3 * D), BF16), mem((D, D), BF16), mem((STEPS, D), BF16),
        mem((STEPS, 3 * D), BF16), mem((HEADS, STEPS, STEPS), BF16), mem((STEPS, D), BF16),
        mem((4, 256, 256), BF16), mem((1024, 256), BF16), mem((1024, 256), BF16),
        mem((STEPS, D), BF16),
        mem((2, 2, 2, 2, 8, 64, 256), BF16), mem((8, *tile), F32), mem((8, *tile), F32),
        mem((2, 4, *tile), F32), mem((8, 2, *tile), F32), mem((128, D), BF16),
        mem((STEPS, D), BF16), mem((2, D, STEPS), BF16), mem((2, STEPS, D), BF16),
        mem((HEADS, 2, 128, 128), F32), mem((2, STEPS, D), BF16), mem((STEPS, D), BF16),
        mem((HEADS, STEPS), F32), mem((STEPS, D), F32), mem((256, 1024), BF16),
        mem((1024, 256), BF16), mem((1024, 256), BF16), mem((STEPS, D), BF16),
        mem((2, 2, 2, 8, 64, 256), BF16), mem((2, 2, 2, 4, 16, 256), BF16),
        mem((2, 4, 64, 256), BF16), mem((2, 2, 2, 8, 16, 256), BF16), mem((2, 8, 64, 256), BF16), mem((2, 2, 8, 16, 256), BF16), mem((8, 64, 256), BF16),
        mem((3, 8, 16, 256), BF16), mem((3, 8, 16, 256), BF16), mem((2, 8, 16, 256), BF16),
        mem((7, 2, 16, 256), BF16), mem((4, 2, 16, 256), F32),
        mem((8, 2, *tile), F32), mem((7, 2, *tile), F32), mem((2, *tile), F32),
        mem((7, *tile), F32), mem(tile, F32), mem((3, *tile), F32), mem(tile, F32),
        mem((7, *tile), F32), mem(tile, F32), mem((7, *tile), F32),
        dma((8,)), dma((32,)), dma((32,)), dma((1,)), dma((1,)), dma((1,)), dma((1,)),
        dma((59,)), dma((59,)), dma((28,)), dma((28,)),
    ]
    shapes = (
            jax.ShapeDtypeStruct((4, AGENTS), F32),
            jax.ShapeDtypeStruct((STEPS, D), BF16),
            jax.ShapeDtypeStruct((16, 3 * D), F32),
            jax.ShapeDtypeStruct((16, D), F32),
    )
    results = pl.pallas_call(
        kernel,
        out_shape=shapes,
        in_specs=[away, vmem, vmem, vmem, vmem, away, away, vmem, vmem, vmem, vmem],
        out_specs=(vmem, vmem, vmem, vmem),
        scratch_shapes=scratch,
        compiler_params=pltpu.CompilerParams(
            collective_id=0, has_side_effects=True, vmem_limit_bytes=60 * 2**20
        ),
    )(
        hidden[0, 0], done_step, alive[0].T, targets[0].T, gain_t[None], w_qkv_t, w_out_t, gain_a[None], w_qkv_a,
        w_out_a, w_value[None],
    )
    values, input_grad, qkv_grad, out_grad = pl.pallas_call(
        hand_on, out_shape=shapes, in_specs=[vmem] * 4, out_specs=(vmem,) * 4
    )(*results)
    return values.T[None], input_grad[None, None], qkv_grad, out_grad


def solution(mesh):
    in_specs = (
        P("env", "tm", None, None),
        P("env", "tm"),
        P("env", None, "tm"),
        P("env", None, "tm"),
        P(),
        P(),
        P(),
        P(),
        P("tm", None),
        P("tm", None),
        P(),
    )
    out_specs = (P("env", None, "tm"), P("env", "tm", None, None), P("tm", None), P("tm", None))
    return jax.shard_map(
        per_device, mesh=mesh, in_specs=in_specs, out_specs=out_specs, check_vma=False
    )
```
